512 devices in a mesh: dp: 16 (over x_lo, y, core), expert: 32 (over x_hi, z).
Axes of the slice: x: 4 (x_hi: 2, x_lo: 2; x = x_hi * 2 + x_lo), y: 4, z: 16, core: 2. Of those that a mesh axis runs over, the one named last changes fastest.
Arguments:
- tokens: bfloat16 [65536, 1024], P(('dp', 'expert')), may hold values from -6 to 6
- routes: int32 [65536, 8], P(('dp', 'expert')), may hold values from 0 to 63, all different within a row; in each aligned block of 128 rows (0 to 127, 128 to 255, ...) at most 17 rows name the same one
- gates: float32 [65536, 8], P(('dp', 'expert')), may hold values from 0.05 to 0.25
- out_grad: bfloat16 [65536, 1024], P(('dp', 'expert')), may hold values from -24 to 24
- w_gate: bfloat16 [64, 1024, 384], P('expert', 'dp'), may hold values from -0.1875 to 0.1875
- w_up: bfloat16 [64, 1024, 384], P('expert', 'dp'), may hold values from -0.1875 to 0.1875
- w_down: bfloat16 [64, 384, 1024], P('expert', None, 'dp'), may hold values from -0.3125 to 0.3125
Outputs:
- mixed: bfloat16 [65536, 1024], P(('dp', 'expert'))
- input_grad: bfloat16 [65536, 1024], P(('dp', 'expert'))
- gate_grad: float32 [65536, 8], P(('dp', 'expert'))
- down_grad: float32 [64, 384, 1024], P('expert', None, 'dp')
The draws below stay inside these ranges and needn't reach their ends.
Inputs may be any that keep to these rules, and one draw needn't show every extreme that they name: `routes`: each row names 8 different experts. Among the 128 rows of one device no expert is named more than 17 times, and in every draw some device names some expert exactly 17 times.
All inputs are finite; a program needn't handle non-finite values.
Results may differ from the reference program's by a relative error of at most 0.022.
Values may be sent and summed in bfloat16 or wider, within the bound.
No kernel may reach another device: no remote copies, remote signals or barrier semaphores. Data moves between devices by JAX's collectives and lax.ppermute only.
A program may use at most 64 MiB of HBM per device.

```python
import math
import jax
import jax.numpy as jnp
import numpy as np
from jax import lax

D = 1024
F = 384
TOP = 8
TOK_DEV = 128
EXPERTS = 64
CAP = 17
TOKENS = 65536
N_DP = 16
N_EXPERT = 32


def strengthened(entries, stream_key, source, target, parts, factor):
    def block_of(dim):
        return (jnp.arange(entries.shape[dim]) // (entries.shape[dim] // parts)).reshape((-1,) + (1,) * (entries.ndim - 1 - dim))

    one_side = jax.random.permutation(stream_key, parts)[block_of(target)]
    far = (block_of(target) + parts // 2) % parts
    return jnp.where((block_of(source) == one_side) | (block_of(source) == far), factor * entries, entries)


def block_scale(own_key, extent, cuts, least, top_value):
    factor_of, own = 1.0, jax.random.fold_in(own_key, 6)
    for dim, blocks in cuts:
        steps = jnp.exp(jax.random.uniform(jax.random.fold_in(own, dim), (blocks,), jnp.float32, least / len(cuts), top_value / len(cuts)))
        factor_of = factor_of * jnp.repeat(steps, extent[dim] // blocks).reshape([-1 if axis == dim else 1 for axis in range(len(extent))])
    return factor_of


def assign_block(rng, own, number, rows, amount, top, most, skew):
    order = jax.random.permutation(rng, amount)
    packed, ordinary = portions_of(amount, rows * top, most, skew, True), portions_of(amount, rows * top, most, skew, False)
    places = jnp.arange(amount)

    def named(tallies, offset_by):
        used = int((tallies > 0).sum())
        fixed = max(1, used // 4)
        passed = fixed + (places - fixed + offset_by * (used - fixed)) % max(1, amount - fixed)
        return jnp.zeros((amount,), jnp.int32).at[order[jnp.where(places < fixed, places, passed)]].set(jnp.asarray(tallies, jnp.int32))

    tallies = jnp.where(number % 4 == 0, named(packed, number // 4), named(ordinary, number - number // 4 - 1))
    mixed = jax.random.permutation(jax.random.fold_in(own, 3), amount)
    source_of, sink = mixed[0:amount // 2 * 2:2], mixed[1:amount // 2 * 2:2]
    margin = jnp.minimum(tallies[source_of] - 1, most - tallies[sink]) // 2
    margin = jnp.where((source_of == order[0]) | (sink == order[0]) | (tallies[sink] == 0), 0, jnp.maximum(margin, 0))
    passed = jax.random.randint(jax.random.fold_in(own, 4), (amount // 2,), 0, 1 << 20) % (margin + 1)
    tallies = tallies.at[source_of].add(-passed).at[sink].add(passed)
    labels = jnp.searchsorted(jnp.cumsum(tallies), jnp.arange(rows * top), side="right").astype(jnp.int32)
    listing = labels.reshape(top, rows).T
    listing = listing[jax.random.permutation(jax.random.fold_in(own, 1), rows)]
    offset_by = jax.random.randint(jax.random.fold_in(own, 2), (rows, 1), 0, top)
    return jnp.take_along_axis(listing, (jnp.arange(top)[None, :] + offset_by) % top, axis=1)


def portions_of(number_of, total, most, lean, full):
    portions = [(1 << 20) // math.isqrt(standing ** lean) + 1 for standing in range(1, number_of + 1)]
    largest = most if full else min(most, max(-(-total // number_of), total * portions[0] // sum(portions)))
    least = 1 if total - largest >= number_of - 1 else 0
    counts, surplus = [largest] + [least] * (number_of - 1), total - largest - least * (number_of - 1)
    while surplus > 0:
        candidates = [i for i in range(1, number_of) if counts[i] < largest] or [i for i in range(1, number_of) if counts[i] < most]
        pool, left = sum([portions[i] for i in candidates]), surplus
        for i in candidates:
            addition = min(most - counts[i], max(1, left * portions[i] // pool), surplus)
            counts[i] = counts[i] + addition
            surplus = surplus - addition
    return np.array(counts)


def bell_draw(own_key, shape, deviation, bound, shards=(), kind=jnp.bfloat16):
    factor_of = block_scale(own_key, shape, shards, -0.22, 0.18) if shards else 1.0
    values = jax.random.normal(own_key, shape, jnp.float32) * deviation * factor_of
    return jnp.minimum(jnp.maximum(values, -bound), bound).astype(kind)


def heavy_noise(rng, dims, scale, reach, shards, heavy, held_as=jnp.bfloat16):
    entries = scale * jax.random.normal(rng, dims, jnp.float32)
    if shards:
        entries = entries * block_scale(rng, dims, shards, -0.22, 0.18)
    return jnp.clip(strengthened(entries, jax.random.fold_in(rng, 3), *heavy), -reach, reach).astype(held_as)


def setup_inputs(seed: int = 0) -> dict:
    seeds = jax.random.split(jax.random.key(seed), 8)
    tokens = bell_draw(seeds[0], (TOKENS, D), 1.0, 6.0, ((0, 512),))
    routes_keys = jax.random.split(jax.random.fold_in(seeds[1], 1), TOKENS // TOK_DEV)
    routes_turns = jax.random.permutation(jax.random.fold_in(seeds[1], 3), TOKENS // TOK_DEV)
    routes = jax.vmap(lambda own, number: assign_block(jax.random.fold_in(seeds[1], 2), own, number, TOK_DEV, EXPERTS, TOP, CAP, 2))(routes_keys, routes_turns).reshape((TOKENS, TOP))
    gates = jnp.clip(0.05 + 0.2 * jax.random.uniform(seeds[2], (TOKENS, TOP), jnp.float32) ** block_scale(seeds[2], (TOKENS, TOP), ((0, 512),), -0.2, 0.2), 0.05, 0.25)
    out_grad = heavy_noise(seeds[3], (TOKENS, D), 1.0, 24.0, ((0, 512),), (0, 1, 512, 6.0))
    w_gate = bell_draw(seeds[4], (EXPERTS, D, F), D ** -0.5, 0.1875, ((0, 32), (1, 16)))
    w_up = bell_draw(seeds[5], (EXPERTS, D, F), D ** -0.5, 0.1875, ((0, 32), (1, 16)))
    w_down = bell_draw(seeds[6], (EXPERTS, F, D), F ** -0.5, 0.3125, ((0, 32), (2, 16)))
    return dict(tokens=tokens, routes=routes, gates=gates, out_grad=out_grad, w_gate=w_gate, w_up=w_up, w_down=w_down)


def slot_ranks(id_row):
    matches = (id_row[:, None] == jnp.arange(EXPERTS, dtype=jnp.int32)[None, :]).astype(jnp.int32)
    return jnp.sum((jnp.cumsum(matches, axis=0) - 1) * matches, axis=1).astype(jnp.int32)


def reference(tokens, routes, gates, out_grad, w_gate, w_up, w_down):
    assigned = TOKENS * TOP
    blocks = TOKENS // TOK_DEV
    per_block = TOK_DEV * TOP
    flat_ids = routes.reshape(blocks, per_block).astype(jnp.int32)
    slots = jax.vmap(slot_ranks)(flat_ids)
    block_ids = jnp.arange(blocks, dtype=jnp.int32)[:, None] * jnp.ones((1, per_block), jnp.int32)
    assign = jnp.arange(assigned, dtype=jnp.int32).reshape(blocks, per_block)
    slot_table = jnp.full((EXPERTS, blocks, CAP), assigned, jnp.int32)
    slot_table = slot_table.at[flat_ids, block_ids, slots].set(assign)
    slot_table = slot_table.reshape(EXPERTS, blocks * CAP)
    tok_pad = jnp.concatenate([tokens, jnp.zeros((1, D), tokens.dtype)], axis=0)
    grad_pad = jnp.concatenate([out_grad, jnp.zeros((1, D), out_grad.dtype)], axis=0)
    gate_pad = jnp.concatenate([gates.reshape(assigned), jnp.zeros((1,), jnp.float32)], axis=0)
    group_rows = N_EXPERT * CAP

    def expert_step(totals, inputs):
        mix_acc, input_acc, gate_acc = totals
        slot_index, gate_weight, up_weight, down_weight = inputs
        tok_index = (slot_index // TOP).astype(jnp.int32)
        rows_in = tok_pad[tok_index]
        grad_rows = grad_pad[tok_index].astype(jnp.float32)
        row_gate = gate_pad[slot_index]
        pre_gate = jnp.dot(rows_in, gate_weight, preferred_element_type=jnp.float32)
        pre_up = jnp.dot(rows_in, up_weight, preferred_element_type=jnp.float32)
        squash = jax.nn.sigmoid(pre_gate)
        active = pre_gate * squash
        hidden = (active * pre_up).astype(jnp.bfloat16)
        expert_out = jnp.dot(hidden, down_weight, preferred_element_type=jnp.float32).astype(jnp.bfloat16)
        out_float = lax.optimization_barrier(expert_out).astype(jnp.float32)
        mix_acc = mix_acc.at[tok_index].add(row_gate[:, None] * out_float, mode="drop")
        gate_acc = gate_acc.at[slot_index].set(jnp.sum(grad_rows * out_float, axis=1), mode="drop")
        out_piece = (row_gate[:, None] * grad_rows).astype(jnp.bfloat16)
        hidden_grad = jnp.dot(out_piece, down_weight.T, preferred_element_type=jnp.float32)
        gate_pre_grad = (hidden_grad * pre_up * squash * (1.0 + pre_gate * (1.0 - squash))).astype(jnp.bfloat16)
        up_pre_grad = (hidden_grad * active).astype(jnp.bfloat16)
        piece_grad = (jnp.dot(gate_pre_grad, gate_weight.T, preferred_element_type=jnp.float32)
                      + jnp.dot(up_pre_grad, up_weight.T, preferred_element_type=jnp.float32)).astype(jnp.bfloat16)
        input_acc = input_acc.at[tok_index].add(lax.optimization_barrier(piece_grad).astype(jnp.float32), mode="drop")
        hid_groups = lax.optimization_barrier(hidden).reshape(N_DP, group_rows, F).astype(jnp.float32)
        piece_groups = lax.optimization_barrier(out_piece).reshape(N_DP, group_rows, D).astype(jnp.float32)
        group_grad = jnp.einsum("gri,grd->gid", hid_groups, piece_groups).astype(jnp.bfloat16)
        down_sum = jnp.sum(lax.optimization_barrier(group_grad).astype(jnp.float32), axis=0)
        return (mix_acc, input_acc, gate_acc), down_sum

    start = (jnp.zeros((TOKENS, D), jnp.float32), jnp.zeros((TOKENS, D), jnp.float32),
             jnp.zeros((assigned,), jnp.float32))
    totals, down_grad = lax.scan(expert_step, start, (slot_table, w_gate, w_up, w_down))
    mix_acc, input_acc, gate_acc = totals
    mixed = mix_acc.astype(jnp.bfloat16)
    input_grad = input_acc.astype(jnp.bfloat16)
    gate_grad = gate_acc.reshape(TOKENS, TOP)
    return mixed, input_grad, gate_grad, down_grad
```

```python
import jax
import jax.numpy as jnp
from jax import lax
from jax.sharding import Mesh, PartitionSpec as P

DP = ("xl", "y", "c")
PLANE = ("xl", "y", "c", "xh")
BLOCKS = ("xl", "y", "c", "xh", "z")


def swap(values, axes):
    return lax.all_to_all(values, axes, split_axis=0, concat_axis=0, tiled=True)


def per_device(tokens, routes, gates, out_grad, w_gate, w_up, w_down):
    plane_devs = lax.axis_size(PLANE)
    dp_devs = lax.axis_size(DP)
    halves = lax.axis_size("xh")
    depth = lax.axis_size("z")
    tok_rows, width = tokens.shape
    top_count = routes.shape[1]
    members, slice_rows, hidden_units = w_gate.shape
    experts = members * plane_devs
    assigned = tok_rows * top_count
    mean_rows = (assigned + experts - 1) // experts
    capacity = min(tok_rows, mean_rows + (mean_rows + 15) // 16)
    total_slots = members * plane_devs * capacity
    groups = depth // members
    sub = slice_rows // groups

    with jax.named_scope("weights_out"):
        packed = jnp.stack([w_gate, w_up, w_down.transpose(0, 2, 1)])
        packed = packed.reshape(3, members, groups, sub, hidden_units)
        packed = packed.transpose(1, 2, 0, 3, 4).reshape(depth, 3, sub, hidden_units)
        packed = swap(packed, "z")
        packed = swap(packed, DP)
        full = lax.all_gather(packed, "z", axis=0, tiled=True)
        full = full.reshape(members, groups, dp_devs, 3, sub, hidden_units)
        full = full.transpose(3, 0, 2, 1, 4, 5).reshape(3, members, width, hidden_units)

    with jax.named_scope("routing"):
        flat_ids = routes.reshape(assigned)
        matches = (flat_ids[:, None] == jnp.arange(experts, dtype=jnp.int32)[None, :]).astype(
            jnp.bfloat16
        )
        row_index = jnp.arange(assigned, dtype=jnp.int32)
        earlier = (row_index[:, None] > row_index[None, :]).astype(jnp.bfloat16)
        before_count = jnp.dot(earlier, matches, preferred_element_type=jnp.float32)
        slot_rank = jnp.sum(before_count * matches.astype(jnp.float32), axis=1).astype(jnp.int32)
        pair = flat_ids // members
        place = pair % dp_devs * halves + pair // dp_devs
        position = (place * capacity + slot_rank) * members + flat_ids % members
        slot_src = (
            jnp.full((total_slots,), assigned, jnp.int32)
            .at[position]
            .set(jnp.arange(assigned, dtype=jnp.int32))
        )
        tok_src = slot_src // top_count

    def spread(rows):
        rows = rows.reshape(plane_devs * capacity, members, width)
        return swap(rows, PLANE)

    with jax.named_scope("send"):
        tok_pad = jnp.concatenate([tokens, jnp.zeros((1, width), tokens.dtype)], axis=0)
        grad_pad = jnp.concatenate([out_grad, jnp.zeros((1, width), out_grad.dtype)], axis=0)
        gate_pad = jnp.concatenate([gates.reshape(assigned), jnp.zeros((1,), jnp.float32)], axis=0)
        recv_x = spread(tok_pad[tok_src])
        slot_gate = gate_pad[slot_src]
        recv_piece = spread(
            (slot_gate[:, None] * grad_pad[tok_src].astype(jnp.float32)).astype(jnp.bfloat16)
        )

    last = (((1,), (1,)), ((), ()))
    first = (((0,), (0,)), ((), ()))
    f32 = jnp.float32
    outs, grads, parts = [], [], []
    with jax.named_scope("experts"):
        for member in range(members):
            rows = recv_x[:, member]
            piece = recv_piece[:, member]
            gate_w, up_w, down_w = full[0, member], full[1, member], full[2, member]
            pre_gate = jnp.dot(rows, gate_w, preferred_element_type=f32)
            pre_up = jnp.dot(rows, up_w, preferred_element_type=f32)
            squash = jax.nn.sigmoid(pre_gate)
            active = pre_gate * squash
            hidden = (active * pre_up).astype(jnp.bfloat16)
            outs.append(
                lax.dot_general(hidden, down_w, last, preferred_element_type=f32).astype(
                    jnp.bfloat16
                )
            )
            parts.append(
                lax.dot_general(piece, hidden, first, preferred_element_type=f32).astype(
                    jnp.bfloat16
                )
            )
            hidden_grad = jnp.dot(piece, down_w, preferred_element_type=f32)
            gate_pre = (hidden_grad * pre_up * squash * (1.0 + pre_gate * (1.0 - squash))).astype(
                jnp.bfloat16
            )
            up_pre = (hidden_grad * active).astype(jnp.bfloat16)
            grads.append(
                (
                    lax.dot_general(gate_pre, gate_w, last, preferred_element_type=f32)
                    + lax.dot_general(up_pre, up_w, last, preferred_element_type=f32)
                ).astype(jnp.bfloat16)
            )
        back_out = swap(jnp.stack(outs, axis=1), PLANE)
        back_grad = swap(jnp.stack(grads, axis=1), PLANE)

    with jax.named_scope("down_grad"):
        part = jnp.stack(parts).reshape(members, dp_devs, groups, sub, hidden_units)
        part = part.transpose(0, 2, 1, 3, 4).reshape(depth, dp_devs, sub, hidden_units)
        part = lax.psum_scatter(part, "z", scatter_dimension=0, tiled=True)
        part = swap(part.reshape(dp_devs, sub, hidden_units), DP)
        part = swap(part, "z")
        down_grad = part.reshape(members, slice_rows, hidden_units).transpose(0, 2, 1).astype(f32)

    with jax.named_scope("combine"):
        assign_out = back_out.reshape(total_slots, width)[position].reshape(
            tok_rows, top_count, width
        )
        mixed = jnp.sum(gates[:, :, None] * assign_out.astype(f32), axis=1).astype(jnp.bfloat16)
        gate_grad = jnp.einsum("tkd,td->tk", assign_out, out_grad, preferred_element_type=f32)
        assign_grad = back_grad.reshape(total_slots, width)[position].reshape(
            tok_rows, top_count, width
        )
        input_grad = jnp.sum(assign_grad, axis=1, dtype=f32).astype(jnp.bfloat16)
    return (mixed, input_grad, gate_grad, down_grad)


def solution(mesh):
    fine = Mesh(mesh.devices.reshape(2, 4, 2, 2, 16), BLOCKS)
    rows = P(BLOCKS, None)
    return jax.shard_map(
        per_device,
        mesh=fine,
        in_specs=(
            rows,
            rows,
            rows,
            rows,
            P(("xh", "z"), DP, None),
            P(("xh", "z"), DP, None),
            P(("xh", "z"), None, DP),
        ),
        out_specs=(rows, rows, rows, P(("xh", "z"), None, DP)),
        check_vma=False,
    )
```

```python
import functools

import jax
import jax.numpy as jnp
from jax import lax
from jax.experimental import pallas as pl
from jax.experimental.pallas import tpu as pltpu
from jax.sharding import Mesh, PartitionSpec as P

DP = ("xl", "y", "c")
PLANE = ("xl", "y", "c", "xh")
BLOCKS = ("xl", "y", "c", "xh", "z")

MAIN = 16
TAIL = 8
F32 = jnp.float32
BF16 = jnp.bfloat16
LAST = (((1,), (1,)), ((), ()))
FIRST = (((0,), (0,)), ((), ()))


def swap(values, axes):
    return lax.all_to_all(values, axes, split_axis=0, concat_axis=0, tiled=True)


def picks(routes_t, gates_t, expert, slot, allowed):
    rows, toks = expert.shape
    match = jnp.zeros((rows, toks), F32)
    gate = jnp.zeros((rows, toks), F32)
    for k in range(routes_t.shape[0]):
        hit = expert == routes_t[k : k + 1, :]
        match = jnp.where(hit, 1.0, match)
        gate = jnp.where(hit, gates_t[k : k + 1, :], gate)
    before = lax.broadcasted_iota(jnp.int32, (toks, toks), 0) < lax.broadcasted_iota(
        jnp.int32, (toks, toks), 1
    )
    rank = jnp.dot(match.astype(BF16), before.astype(BF16), preferred_element_type=F32)
    chosen = (match > 0.5) & (rank.astype(jnp.int32) == slot) & allowed
    return chosen, jnp.where(chosen, gate, 0.0)


def main_rows(toks, devs, halves, members):
    rows = devs * members * MAIN
    row = lax.broadcasted_iota(jnp.int32, (rows, toks), 0)
    dev = row // (members * MAIN)
    member = row % (members * MAIN) // MAIN
    expert = (dev % halves * (devs // halves) + dev // halves) * members + member
    return expert, row % MAIN


def tail_rows(toks, devs, halves, members):
    row = lax.broadcasted_iota(jnp.int32, (devs * TAIL, toks), 0)
    dev, place = row // TAIL, row % TAIL
    expert = (dev % halves * (devs // halves) + dev // halves) * members + place % members
    return expert, place // members


def send_kernel(halves, members, routes_ref, gates_ref, tok_ref, grad_ref, x_ref, p_ref):
    devs, _, width = x_ref.shape
    toks = tok_ref.shape[0]
    routes_t, gates_t = routes_ref[...], gates_ref[...]
    tok, grad = tok_ref[...], grad_ref[...]
    expert, slot = main_rows(toks, devs, halves, members)
    chosen, gate = picks(routes_t, gates_t, expert, slot, True)
    hot = chosen.astype(F32).astype(BF16)
    scale = jnp.sum(gate, axis=1, keepdims=True)
    x_ref[...] = jnp.dot(hot, tok, preferred_element_type=F32).astype(BF16).reshape(x_ref.shape)
    rows = scale * jnp.dot(hot, grad, preferred_element_type=F32)
    p_ref[:, : members * MAIN, :] = rows.astype(BF16).reshape(devs, members * MAIN, width)
    expert, kind = tail_rows(toks, devs, halves, members)
    chosen, gate = picks(routes_t, gates_t, expert, MAIN, kind < 2)
    hot = chosen.astype(F32)
    scale = jnp.sum(gate, axis=1, keepdims=True)
    hot_x = jnp.where(kind == 0, hot, 0.0).astype(BF16)
    hot_p = jnp.where(kind == 1, hot, 0.0).astype(BF16)
    rows = jnp.dot(hot_x, tok, preferred_element_type=F32) + scale * jnp.dot(
        hot_p, grad, preferred_element_type=F32
    )
    p_ref[:, members * MAIN :, :] = rows.astype(BF16).reshape(devs, TAIL, width)


def tail_order(devs, members):
    shape = (2 * members * devs, devs * TAIL)
    row = lax.broadcasted_iota(jnp.int32, shape, 0)
    col = lax.broadcasted_iota(jnp.int32, shape, 1)
    return (col == row % devs * TAIL + row // devs).astype(F32).astype(BF16)


def expert_kernel(members, x_ref, p_ref, w_ref, out_ref, tail_ref, part_ref, gp_ref, up_ref):
    devs, _, width = x_ref.shape
    side = members * MAIN
    tails = jnp.dot(
        tail_order(devs, members),
        p_ref[:, side:, :].reshape(devs * TAIL, width),
        preferred_element_type=F32,
    ).astype(BF16)
    for member in range(members):
        here = slice(member * MAIN, (member + 1) * MAIN)
        extra = slice(member * devs, (member + 1) * devs)
        extra_p = slice((members + member) * devs, (members + member + 1) * devs)
        rows = jnp.concatenate(
            [x_ref[:, here, :].reshape(devs * MAIN, width), tails[extra]], axis=0
        )
        piece = jnp.concatenate(
            [p_ref[:, here, :].reshape(devs * MAIN, width), tails[extra_p]], axis=0
        )
        down_w = w_ref[2, member]
        pre_gate = jnp.dot(rows, w_ref[0, member], preferred_element_type=F32)
        pre_up = jnp.dot(rows, w_ref[1, member], preferred_element_type=F32)
        squash = 1.0 / (1.0 + jnp.exp(-pre_gate))
        active = pre_gate * squash
        hidden = (active * pre_up).astype(BF16)
        part_ref[member] = lax.dot_general(
            piece, hidden, FIRST, preferred_element_type=F32
        ).astype(BF16)
        out = lax.dot_general(hidden, down_w, LAST, preferred_element_type=F32).astype(BF16)
        out_ref[:, here, :] = out[: devs * MAIN].reshape(devs, MAIN, width)
        tail_ref[extra] = out[devs * MAIN :]
        hidden_grad = jnp.dot(piece, down_w, preferred_element_type=F32)
        gp_ref[member] = (
            hidden_grad * pre_up * squash * (1.0 + pre_gate * (1.0 - squash))
        ).astype(BF16)
        up_ref[member] = (hidden_grad * active).astype(BF16)


def input_kernel(members, gp_ref, up_ref, w_ref, tail_ref, out_ref):
    devs, _, width = out_ref.shape
    side = members * MAIN
    tails = []
    for member in range(members):
        grad = (
            lax.dot_general(gp_ref[member], w_ref[0, member], LAST, preferred_element_type=F32)
            + lax.dot_general(up_ref[member], w_ref[1, member], LAST, preferred_element_type=F32)
        ).astype(BF16)
        out_ref[:, member * MAIN : (member + 1) * MAIN, :] = grad[: devs * MAIN].reshape(
            devs, MAIN, width
        )
        tails.append(grad[devs * MAIN :])
    tails = jnp.concatenate([tail_ref[...]] + tails, axis=0)
    out_ref[:, side:, :] = (
        lax.dot_general(tail_order(devs, members), tails, FIRST, preferred_element_type=F32)
        .astype(BF16)
        .reshape(devs, TAIL, width)
    )


def combine_kernel(
    halves, members, routes_ref, gates_ref, grad_ref, out_ref, back_ref, mix_ref, in_ref, gg_ref
):
    devs, side, width = out_ref.shape
    toks = grad_ref.shape[0]
    routes_t, gates_t = routes_ref[...], gates_ref[...]
    og = grad_ref[...]

    def split(values):
        high = values.astype(BF16)
        return high, (values - high.astype(F32)).astype(BF16)

    expert, slot = main_rows(toks, devs, halves, members)
    chosen, gate = picks(routes_t, gates_t, expert, slot, True)
    hot = chosen.astype(F32).astype(BF16)
    expert_t, kind = tail_rows(toks, devs, halves, members)
    chosen_t, gate_t = picks(routes_t, gates_t, expert_t, MAIN, kind < 2)
    hot_g = jnp.where(kind == 1, chosen_t.astype(F32), 0.0).astype(BF16)
    chosen_t = chosen_t & (kind == 0)
    gate_t = jnp.where(kind == 0, gate_t, 0.0)

    def gather(weights, rows):
        return lax.dot_general(weights, rows, FIRST, preferred_element_type=F32)

    out = out_ref[...].reshape(devs * side, width)
    back = back_ref[:, :side, :].reshape(devs * side, width)
    tail = back_ref[:, side:, :].reshape(devs * TAIL, width)
    high, low = split(gate)
    high_t, low_t = split(gate_t)
    mix_ref[...] = (
        gather(high, out) + gather(low, out) + gather(high_t, tail) + gather(low_t, tail)
    ).astype(BF16)
    in_ref[...] = (gather(hot, back) + gather(hot_g, tail)).astype(BF16)
    score = jnp.where(chosen, lax.dot_general(out, og, LAST, preferred_element_type=F32), 0.0)
    score_t = jnp.where(chosen_t, lax.dot_general(tail, og, LAST, preferred_element_type=F32), 0.0)
    for k in range(routes_t.shape[0]):
        line = routes_t[k : k + 1, :]
        gg_ref[k : k + 1, :] = jnp.sum(
            jnp.where(expert == line, score, 0.0), axis=0, keepdims=True
        ) + jnp.sum(jnp.where(expert_t == line, score_t, 0.0), axis=0, keepdims=True)


def call(kernel, name, outs, flops, args):
    flat = outs if isinstance(outs, tuple) else (outs,)
    total = sum(a.size * a.dtype.itemsize for a in (*args, *flat))
    return pl.pallas_call(
        kernel,
        name=name,
        out_shape=outs,
        compiler_params=pltpu.CompilerParams(vmem_limit_bytes=56 << 20),
        cost_estimate=pl.CostEstimate(flops=flops, bytes_accessed=total, transcendentals=0),
    )(*args)


def per_device(tokens, routes, gates, out_grad, w_gate, w_up, w_down):
    devs = lax.axis_size(PLANE)
    dp_devs = lax.axis_size(DP)
    halves = lax.axis_size("xh")
    depth = lax.axis_size("z")
    toks, width = tokens.shape
    members, slice_rows, hidden_units = w_gate.shape
    groups = depth // members
    sub = slice_rows // groups
    side = members * MAIN
    slots = devs * (MAIN + 1)
    shape = jax.ShapeDtypeStruct

    with jax.named_scope("weights_out"):
        packed = jnp.stack([w_gate, w_up, w_down.transpose(0, 2, 1)])
        packed = packed.reshape(3, members, groups, sub, hidden_units)
        packed = packed.transpose(1, 2, 0, 3, 4).reshape(depth, 3, sub, hidden_units)
        packed = swap(packed, "z")

    with jax.named_scope("send"):
        routes_t, gates_t = routes.T, gates.T
        send_x, send_p = call(
            functools.partial(send_kernel, halves, members),
            "send",
            (shape((devs, side, width), BF16), shape((devs, side + TAIL, width), BF16)),
            4 * slots * members * toks * width,
            (routes_t, gates_t, tokens, out_grad),
        )

    with jax.named_scope("weights_in"):
        packed, send_x, send_p = lax.optimization_barrier((packed, send_x, send_p))
        packed = swap(packed, DP)
        full = lax.all_gather(packed, "z", axis=0, tiled=True)
        full = full.reshape(members, groups, dp_devs, 3, sub, hidden_units)
        full = full.transpose(3, 0, 2, 1, 4, 5).reshape(3, members, width, hidden_units)

    with jax.named_scope("exchange"):
        send_x, packed = lax.optimization_barrier((send_x, packed))
        recv_x = swap(send_x, PLANE)
        send_p, recv_x = lax.optimization_barrier((send_p, recv_x))
        recv_p = swap(send_p, PLANE)

    with jax.named_scope("experts"):
        unit = 2 * slots * members * width * hidden_units
        out, tail, part, gate_pre, up_pre = call(
            functools.partial(expert_kernel, members),
            "experts",
            (
                shape((devs, side, width), BF16),
                shape((members * devs, width), BF16),
                shape((members, width, hidden_units), BF16),
                shape((members, slots, hidden_units), BF16),
                shape((members, slots, hidden_units), BF16),
            ),
            5 * unit,
            (recv_x, recv_p, full),
        )
        back_out = swap(out, PLANE)
        grad = call(
            functools.partial(input_kernel, members),
            "input_grad",
            shape((devs, side + TAIL, width), BF16),
            2 * unit,
            (gate_pre, up_pre, full, tail),
        )
        grad, back_out = lax.optimization_barrier((grad, back_out))
        back_grad = swap(grad, PLANE)

    with jax.named_scope("down_grad"):
        part = part.reshape(members, dp_devs, groups, sub, hidden_units)
        part = part.transpose(0, 2, 1, 3, 4).reshape(depth, dp_devs, sub, hidden_units)
        part = lax.psum_scatter(part, "z", scatter_dimension=0, tiled=True)
        part, back_grad = lax.optimization_barrier((part, back_grad))
        part = swap(part.reshape(dp_devs, sub, hidden_units), DP)
        part = swap(part, "z")
        down_grad = part.reshape(members, slice_rows, hidden_units).transpose(0, 2, 1).astype(F32)

    with jax.named_scope("combine"):
        mixed, input_grad, gate_grad = call(
            functools.partial(combine_kernel, halves, members),
            "combine",
            (
                shape((toks, width), BF16),
                shape((toks, width), BF16),
                shape(routes_t.shape, F32),
            ),
            8 * slots * members * toks * width,
            (routes_t, gates_t, out_grad, back_out, back_grad),
        )
    return (mixed, input_grad, gate_grad.T, down_grad)


def solution(mesh):
    fine = Mesh(mesh.devices.reshape(2, 4, 2, 2, 16), BLOCKS)
    rows = P(BLOCKS, None)
    return jax.shard_map(
        per_device,
        mesh=fine,
        in_specs=(
            rows,
            rows,
            rows,
            rows,
            P(("xh", "z"), DP, None),
            P(("xh", "z"), DP, None),
            P(("xh", "z"), None, DP),
        ),
        out_specs=(rows, rows, rows, P(("xh", "z"), None, DP)),
        check_vma=False,
    )
```

```python
import functools

import jax
import jax.numpy as jnp
from jax import lax
from jax.experimental import pallas as pl
from jax.experimental.pallas import tpu as pltpu
from jax.sharding import Mesh, PartitionSpec as P

DP = ("xl", "y", "c")
PLANE = ("xl", "y", "c", "xh")
BLOCKS = ("xl", "y", "c", "xh", "z")

MAIN = 16
TAIL = 8
F32 = jnp.float32
BF16 = jnp.bfloat16
LAST = (((1,), (1,)), ((), ()))
FIRST = (((0,), (0,)), ((), ()))


def swap(values, axes):
    return lax.all_to_all(values, axes, split_axis=0, concat_axis=0, tiled=True)


def picks(routes_t, gates_t, expert, slot, allowed):
    rows, toks = expert.shape
    match = jnp.zeros((rows, toks), F32)
    gate = jnp.zeros((rows, toks), F32)
    for k in range(routes_t.shape[0]):
        hit = expert == routes_t[k : k + 1, :]
        match = jnp.where(hit, 1.0, match)
        gate = jnp.where(hit, gates_t[k : k + 1, :], gate)
    before = lax.broadcasted_iota(jnp.int32, (toks, toks), 0) < lax.broadcasted_iota(
        jnp.int32, (toks, toks), 1
    )
    rank = jnp.dot(match.astype(BF16), before.astype(BF16), preferred_element_type=F32)
    chosen = (match > 0.5) & (rank.astype(jnp.int32) == slot) & allowed
    return chosen, jnp.where(chosen, gate, 0.0)


def expert_of(dev, member, devs, halves, cores, members):
    cell = dev // halves
    depth = devs // halves
    pair = dev % halves * depth + cell % cores * (depth // cores) + cell // cores
    return pair * members + member


def main_rows(toks, devs, halves, cores, members):
    rows = devs * members * MAIN
    row = lax.broadcasted_iota(jnp.int32, (rows, toks), 0)
    dev = row // (members * MAIN)
    member = row % (members * MAIN) // MAIN
    return expert_of(dev, member, devs, halves, cores, members), row % MAIN


def tail_rows(toks, devs, halves, cores, members):
    row = lax.broadcasted_iota(jnp.int32, (devs * TAIL, toks), 0)
    dev, place = row // TAIL, row % TAIL
    return expert_of(dev, place % members, devs, halves, cores, members), place // members


def send_kernel(halves, cores, members, routes_ref, gates_ref, tok_ref, grad_ref, x_ref, p_ref):
    devs, _, width = x_ref.shape
    toks = tok_ref.shape[0]
    routes_t, gates_t = routes_ref[...], gates_ref[...]
    tok, grad = tok_ref[...], grad_ref[...]
    expert, slot = main_rows(toks, devs, halves, cores, members)
    chosen, gate = picks(routes_t, gates_t, expert, slot, True)
    hot = chosen.astype(F32).astype(BF16)
    scale = jnp.sum(gate, axis=1, keepdims=True)
    x_ref[...] = jnp.dot(hot, tok, preferred_element_type=F32).astype(BF16).reshape(x_ref.shape)
    rows = scale * jnp.dot(hot, grad, preferred_element_type=F32)
    p_ref[:, : members * MAIN, :] = rows.astype(BF16).reshape(devs, members * MAIN, width)
    expert, kind = tail_rows(toks, devs, halves, cores, members)
    chosen, gate = picks(routes_t, gates_t, expert, MAIN, kind < 2)
    hot = chosen.astype(F32)
    scale = jnp.sum(gate, axis=1, keepdims=True)
    hot_x = jnp.where(kind == 0, hot, 0.0).astype(BF16)
    hot_p = jnp.where(kind == 1, hot, 0.0).astype(BF16)
    rows = jnp.dot(hot_x, tok, preferred_element_type=F32) + scale * jnp.dot(
        hot_p, grad, preferred_element_type=F32
    )
    p_ref[:, members * MAIN :, :] = rows.astype(BF16).reshape(devs, TAIL, width)


def tail_order(devs, members):
    shape = (2 * members * devs, devs * TAIL)
    row = lax.broadcasted_iota(jnp.int32, shape, 0)
    col = lax.broadcasted_iota(jnp.int32, shape, 1)
    return (col == row % devs * TAIL + row // devs).astype(F32).astype(BF16)


def rows_of(ref, tails, member, kind, members):
    devs, _, width = ref.shape
    start = (kind * members + member) * devs
    main = ref[:, member * MAIN : (member + 1) * MAIN, :].reshape(devs * MAIN, width)
    return jnp.concatenate([main, tails[start : start + devs]], axis=0)


def tails_of(p_ref, members):
    devs, _, width = p_ref.shape
    rows = p_ref[:, members * MAIN :, :].reshape(devs * TAIL, width)
    return jnp.dot(tail_order(devs, members), rows, preferred_element_type=F32).astype(BF16)


def fetch(sems, pairs):
    copies = [pltpu.make_async_copy(src, dst, sems.at[i]) for i, (src, dst) in enumerate(pairs)]
    for copy in copies:
        copy.start()
    return copies


def hidden_kernel(members, x_hbm, p_hbm, w_hbm, part_ref, hid_ref, act_ref, slope_ref, *scratch):
    p_ref, x_ref, gate_ref, up_ref, sems = scratch
    width, units = x_ref.shape[2], hid_ref.shape[2]
    copies = fetch(
        sems,
        [(p_hbm, p_ref), (x_hbm, x_ref), (w_hbm.at[:, 0], gate_ref), (w_hbm.at[:, 1], up_ref)],
    )
    copies[0].wait()
    tails = tails_of(p_ref, members)
    for copy in copies[1:]:
        copy.wait()
    for member in range(members):
        rows = rows_of(x_ref, tails, member, 0, members)
        piece = rows_of(p_ref, tails, member, 1, members)
        pre_gate = jnp.dot(
            rows, gate_ref[:, member].reshape(width, units), preferred_element_type=F32
        )
        pre_up = jnp.dot(rows, up_ref[:, member].reshape(width, units), preferred_element_type=F32)
        squash = 1.0 / (1.0 + jnp.exp(-pre_gate))
        active = pre_gate * squash
        hidden = (active * pre_up).astype(BF16)
        hid_ref[member] = hidden
        act_ref[member] = active
        slope_ref[member] = pre_up * squash * (1.0 + pre_gate * (1.0 - squash))
        part = lax.dot_general(piece, hidden, FIRST, preferred_element_type=F32)
        part_ref[:, member] = part.astype(BF16).reshape(part_ref.shape[0], -1, units)


def out_kernel(members, hid_ref, w_hbm, out_ref, tail_ref, down_ref, sems):
    devs, _, width = out_ref.shape
    units = hid_ref.shape[2]
    (copy,) = fetch(sems, [(w_hbm.at[:, 2], down_ref)])
    copy.wait()
    for member in range(members):
        down_w = down_ref[:, member].reshape(width, units)
        out = lax.dot_general(hid_ref[member], down_w, LAST, preferred_element_type=F32)
        out = out.astype(BF16)
        out_ref[:, member * MAIN : (member + 1) * MAIN, :] = out[: devs * MAIN].reshape(
            devs, MAIN, width
        )
        tail_ref[member * devs : (member + 1) * devs] = out[devs * MAIN :]


def input_kernel(members, p_ref, act_ref, slope_ref, tail_ref, w_hbm, out_ref, *scratch):
    down_ref, gate_ref, up_ref, sems = scratch
    devs, _, width = out_ref.shape
    units = act_ref.shape[2]
    copies = fetch(
        sems,
        [(w_hbm.at[:, 2], down_ref), (w_hbm.at[:, 0], gate_ref), (w_hbm.at[:, 1], up_ref)],
    )
    piece_tails = tails_of(p_ref, members)
    for copy in copies:
        copy.wait()
    tails = [tail_ref[...]]
    for member in range(members):
        piece = rows_of(p_ref, piece_tails, member, 1, members)
        down_w = down_ref[:, member].reshape(width, units)
        gate_w = gate_ref[:, member].reshape(width, units)
        up_w = up_ref[:, member].reshape(width, units)
        hidden_grad = jnp.dot(piece, down_w, preferred_element_type=F32)
        gate_pre = (hidden_grad * slope_ref[member]).astype(BF16)
        up_pre = (hidden_grad * act_ref[member]).astype(BF16)
        grad = (
            lax.dot_general(gate_pre, gate_w, LAST, preferred_element_type=F32)
            + lax.dot_general(up_pre, up_w, LAST, preferred_element_type=F32)
        ).astype(BF16)
        out_ref[:, member * MAIN : (member + 1) * MAIN, :] = grad[: devs * MAIN].reshape(
            devs, MAIN, width
        )
        tails.append(grad[devs * MAIN :])
    tails = jnp.concatenate(tails, axis=0)
    out_ref[:, members * MAIN :, :] = (
        lax.dot_general(tail_order(devs, members), tails, FIRST, preferred_element_type=F32)
        .astype(BF16)
        .reshape(devs, TAIL, width)
    )


def combine_kernel(
    halves, cores, members, routes_ref, gates_ref, grad_ref, out_ref, back_ref, mix_ref, in_ref, gg_ref
):
    devs, side, width = out_ref.shape
    toks = grad_ref.shape[0]
    routes_t, gates_t = routes_ref[...], gates_ref[...]
    og = grad_ref[...]

    def split(values):
        high = values.astype(BF16)
        return high, (values - high.astype(F32)).astype(BF16)

    expert, slot = main_rows(toks, devs, halves, cores, members)
    chosen, gate = picks(routes_t, gates_t, expert, slot, True)
    hot = chosen.astype(F32).astype(BF16)
    expert_t, kind = tail_rows(toks, devs, halves, cores, members)
    chosen_t, gate_t = picks(routes_t, gates_t, expert_t, MAIN, kind < 2)
    hot_g = jnp.where(kind == 1, chosen_t.astype(F32), 0.0).astype(BF16)
    chosen_t = chosen_t & (kind == 0)
    gate_t = jnp.where(kind == 0, gate_t, 0.0)

    def gather(weights, rows):
        return lax.dot_general(weights, rows, FIRST, preferred_element_type=F32)

    out = out_ref[...].reshape(devs * side, width)
    back = back_ref[:, :side, :].reshape(devs * side, width)
    tail = back_ref[:, side:, :].reshape(devs * TAIL, width)
    high, low = split(gate)
    high_t, low_t = split(gate_t)
    mix_ref[...] = (
        gather(high, out) + gather(low, out) + gather(high_t, tail) + gather(low_t, tail)
    ).astype(BF16)
    in_ref[...] = (gather(hot, back) + gather(hot_g, tail)).astype(BF16)
    score = jnp.where(chosen, lax.dot_general(out, og, LAST, preferred_element_type=F32), 0.0)
    score_t = jnp.where(chosen_t, lax.dot_general(tail, og, LAST, preferred_element_type=F32), 0.0)
    for k in range(routes_t.shape[0]):
        line = routes_t[k : k + 1, :]
        gg_ref[k : k + 1, :] = jnp.sum(
            jnp.where(expert == line, score, 0.0), axis=0, keepdims=True
        ) + jnp.sum(jnp.where(expert_t == line, score_t, 0.0), axis=0, keepdims=True)


def call(kernel, name, outs, flops, args, anywhere=(), scratch=()):
    flat = outs if isinstance(outs, tuple) else (outs,)
    total = sum(a.size * a.dtype.itemsize for a in (*args, *flat))
    inner = pl.BlockSpec()
    outer = pl.BlockSpec(memory_space=pltpu.HBM)
    return pl.pallas_call(
        kernel,
        name=name,
        out_shape=outs,
        in_specs=[outer if i in anywhere else inner for i in range(len(args))],
        out_specs=tuple(inner for _ in flat) if isinstance(outs, tuple) else inner,
        scratch_shapes=scratch,
        compiler_params=pltpu.CompilerParams(vmem_limit_bytes=60 << 20),
        cost_estimate=pl.CostEstimate(flops=flops, bytes_accessed=total, transcendentals=0),
    )(*args)


def per_device(tokens, routes, gates, out_grad, w_gate, w_up, w_down):
    devs = lax.axis_size(PLANE)
    dp_devs = lax.axis_size(DP)
    halves = lax.axis_size("xh")
    cores = lax.axis_size("c")
    toks, width = tokens.shape
    members, slice_rows, units = w_gate.shape
    side = members * MAIN
    slots = devs * (MAIN + 1)
    shape = jax.ShapeDtypeStruct
    vmem = pltpu.VMEM
    dma = pltpu.SemaphoreType.DMA

    there = []
    for cell in range(dp_devs):
        for plane in range(dp_devs):
            near = dp_devs // cores
            column = plane % near * cores + plane // near
            there.append((cell * dp_devs + plane, column * dp_devs + cell))
    back = [(b, a) for a, b in there]

    with jax.named_scope("weights"):
        packed = jnp.stack([w_gate, w_up, w_down.transpose(0, 2, 1)])
        packed = lax.ppermute(packed, DP + ("z",), there)

    with jax.named_scope("send"):
        routes_t, gates_t = routes.T, gates.T
        send_x, send_p = call(
            functools.partial(send_kernel, halves, cores, members),
            "send",
            (shape((devs, side, width), BF16), shape((devs, side + TAIL, width), BF16)),
            4 * slots * members * toks * width,
            (routes_t, gates_t, tokens, out_grad),
        )
        packed, send_x = lax.optimization_barrier((packed, send_x))
        full = lax.all_gather(packed, "z", axis=0)
        weight = (full.shape[0], members, slice_rows, units)
        recv_x = swap(send_x, PLANE)
        send_p, recv_x = lax.optimization_barrier((send_p, recv_x))
        recv_p = swap(send_p, PLANE)

    unit = 2 * slots * members * width * units
    wide = (members, slots, units)
    with jax.named_scope("hidden"):
        part, hidden, active, slope = call(
            functools.partial(hidden_kernel, members),
            "hidden",
            (shape(weight, BF16), shape(wide, BF16), shape(wide, F32), shape(wide, F32)),
            3 * unit,
            (recv_x, recv_p, full),
            (0, 1, 2),
            (
                vmem(recv_p.shape, BF16),
                vmem(recv_x.shape, BF16),
                vmem(weight, BF16),
                vmem(weight, BF16),
                dma((4,)),
            ),
        )

    with jax.named_scope("down_grad"):
        part = lax.psum_scatter(part, "z", scatter_dimension=0)
        part = lax.ppermute(part, DP + ("z",), back)
        down_grad = part.transpose(0, 2, 1).astype(F32)

    with jax.named_scope("out"):
        out, tail = call(
            functools.partial(out_kernel, members),
            "out",
            (shape((devs, side, width), BF16), shape((members * devs, width), BF16)),
            unit,
            (hidden, full),
            (1,),
            (vmem(weight, BF16), dma((1,))),
        )
        back_out = swap(out, PLANE)

    with jax.named_scope("input_grad"):
        grad = call(
            functools.partial(input_kernel, members),
            "input_grad",
            shape((devs, side + TAIL, width), BF16),
            3 * unit,
            (recv_p, active, slope, tail, full),
            (4,),
            (vmem(weight, BF16), vmem(weight, BF16), vmem(weight, BF16), dma((3,))),
        )
        grad, back_out = lax.optimization_barrier((grad, back_out))
        back_grad = swap(grad, PLANE)

    with jax.named_scope("combine"):
        mixed, input_grad, gate_grad = call(
            functools.partial(combine_kernel, halves, cores, members),
            "combine",
            (
                shape((toks, width), BF16),
                shape((toks, width), BF16),
                shape(routes_t.shape, F32),
            ),
            8 * slots * members * toks * width,
            (routes_t, gates_t, out_grad, back_out, back_grad),
        )
    return (mixed, input_grad, gate_grad.T, down_grad)


def solution(mesh):
    fine = Mesh(mesh.devices.reshape(2, 4, 2, 2, 16), BLOCKS)
    rows = P(BLOCKS, None)
    return jax.shard_map(
        per_device,
        mesh=fine,
        in_specs=(
            rows,
            rows,
            rows,
            rows,
            P(("xh", "z"), DP, None),
            P(("xh", "z"), DP, None),
            P(("xh", "z"), None, DP),
        ),
        out_specs=(rows, rows, rows, P(("xh", "z"), None, DP)),
        check_vma=False,
    )
```

```python
import functools

import jax
import jax.numpy as jnp
from jax import lax
from jax.experimental import pallas as pl
from jax.experimental.pallas import tpu as pltpu
from jax.sharding import Mesh, PartitionSpec as P

DP = ("xl", "y", "c")
PLANE = ("xl", "y", "c", "xh")
BLOCKS = ("xl", "y", "c", "xh", "z")

MAIN = 16
TAIL = 8
F32 = jnp.float32
BF16 = jnp.bfloat16
LAST = (((1,), (1,)), ((), ()))
FIRST = (((0,), (0,)), ((), ()))


def swap(values, axes):
    return lax.all_to_all(values, axes, split_axis=0, concat_axis=0, tiled=True)


def picks(routes_t, gates_t, expert, slot, allowed):
    rows, toks = expert.shape
    match = jnp.zeros((rows, toks), F32)
    gate = jnp.zeros((rows, toks), F32)
    for k in range(routes_t.shape[0]):
        hit = expert == routes_t[k : k + 1, :]
        match = jnp.where(hit, 1.0, match)
        gate = jnp.where(hit, gates_t[k : k + 1, :], gate)
    before = lax.broadcasted_iota(jnp.int32, (toks, toks), 0) < lax.broadcasted_iota(
        jnp.int32, (toks, toks), 1
    )
    rank = jnp.dot(match.astype(BF16), before.astype(BF16), preferred_element_type=F32)
    chosen = (match > 0.5) & (rank.astype(jnp.int32) == slot) & allowed
    return chosen, jnp.where(chosen, gate, 0.0)


def expert_of(dev, member, devs, halves, cores, members):
    cell = dev // halves
    depth = devs // halves
    pair = dev % halves * depth + cell % cores * (depth // cores) + cell // cores
    return pair * members + member


def main_rows(toks, devs, halves, cores, members):
    rows = devs * members * MAIN
    row = lax.broadcasted_iota(jnp.int32, (rows, toks), 0)
    dev = row // (members * MAIN)
    member = row % (members * MAIN) // MAIN
    return expert_of(dev, member, devs, halves, cores, members), row % MAIN


def tail_rows(toks, devs, halves, cores, members):
    row = lax.broadcasted_iota(jnp.int32, (devs * TAIL, toks), 0)
    dev, place = row // TAIL, row % TAIL
    return expert_of(dev, place % members, devs, halves, cores, members), place // members


def send_kernel(halves, cores, members, routes_ref, gates_ref, tok_ref, grad_ref, x_ref, p_ref):
    devs, _, width = x_ref.shape
    toks = tok_ref.shape[0]
    routes_t, gates_t = routes_ref[...], gates_ref[...]
    tok, grad = tok_ref[...], grad_ref[...]
    expert, slot = main_rows(toks, devs, halves, cores, members)
    chosen, gate = picks(routes_t, gates_t, expert, slot, True)
    hot = chosen.astype(F32).astype(BF16)
    scale = jnp.sum(gate, axis=1, keepdims=True)
    x_ref[...] = jnp.dot(hot, tok, preferred_element_type=F32).astype(BF16).reshape(x_ref.shape)
    rows = scale * jnp.dot(hot, grad, preferred_element_type=F32)
    p_ref[:, : members * MAIN, :] = rows.astype(BF16).reshape(devs, members * MAIN, width)
    expert, kind = tail_rows(toks, devs, halves, cores, members)
    chosen, gate = picks(routes_t, gates_t, expert, MAIN, kind < 2)
    hot = chosen.astype(F32)
    scale = jnp.sum(gate, axis=1, keepdims=True)
    hot_x = jnp.where(kind == 0, hot, 0.0).astype(BF16)
    hot_p = jnp.where(kind == 1, hot, 0.0).astype(BF16)
    rows = jnp.dot(hot_x, tok, preferred_element_type=F32) + scale * jnp.dot(
        hot_p, grad, preferred_element_type=F32
    )
    p_ref[:, members * MAIN :, :] = rows.astype(BF16).reshape(devs, TAIL, width)


def tail_order(devs, members):
    shape = (2 * members * devs, devs * TAIL)
    row = lax.broadcasted_iota(jnp.int32, shape, 0)
    col = lax.broadcasted_iota(jnp.int32, shape, 1)
    return (col == row % devs * TAIL + row // devs).astype(F32).astype(BF16)


def rows_of(ref, tails, member, kind, members):
    devs, _, width = ref.shape
    start = (kind * members + member) * devs
    main = ref[:, member * MAIN : (member + 1) * MAIN, :].reshape(devs * MAIN, width)
    return jnp.concatenate([main, tails[start : start + devs]], axis=0)


def tails_of(extra, members):
    devs, _, width = extra.shape
    rows = extra[...].reshape(devs * TAIL, width)
    return jnp.dot(tail_order(devs, members), rows, preferred_element_type=F32).astype(BF16)


def fetch(sems, pairs):
    copies = [pltpu.make_async_copy(src, dst, sems.at[i]) for i, (src, dst) in enumerate(pairs)]
    for copy in copies:
        copy.start()
    return copies


def parts_of(w_hbm, which, ref):
    near, cores = ref.shape[:2]
    return [(w_hbm.at[c * near : (c + 1) * near, which], ref.at[:, c]) for c in range(cores)]


def matrix(ref, member):
    near, cores, _, rows, units = ref.shape
    return ref[:, :, member].reshape(near * cores * rows, units)


def forward_kernel(members, x_hbm, p_hbm, w_hbm, out_ref, tail_ref, hid_ref, *scratch):
    extra_ref, x_ref, gate_ref, up_ref, down_ref, sems = scratch
    devs, _, width = x_ref.shape
    copies = fetch(
        sems,
        [(p_hbm.at[:, members * MAIN :, :], extra_ref), (x_hbm, x_ref)]
        + parts_of(w_hbm, 0, gate_ref)
        + parts_of(w_hbm, 1, up_ref)
        + parts_of(w_hbm, 2, down_ref),
    )
    copies[0].wait()
    tails = tails_of(extra_ref, members)
    copies[1].wait()
    rows = [rows_of(x_ref, tails, member, 0, members) for member in range(members)]
    for copy in copies[2:]:
        copy.wait()
    for member in range(members):
        pre_gate = jnp.dot(rows[member], matrix(gate_ref, member), preferred_element_type=F32)
        pre_up = jnp.dot(rows[member], matrix(up_ref, member), preferred_element_type=F32)
        active = pre_gate / (1.0 + jnp.exp(-pre_gate))
        hidden = (active * pre_up).astype(BF16)
        hid_ref[member] = hidden
        out = lax.dot_general(hidden, matrix(down_ref, member), LAST, preferred_element_type=F32)
        out = out.astype(BF16)
        out_ref[:, member * MAIN : (member + 1) * MAIN, :] = out[: devs * MAIN].reshape(
            devs, MAIN, width
        )
        tail_ref[member * devs : (member + 1) * devs] = out[devs * MAIN :]


def part_kernel(members, cores, p_ref, hid_ref, part_ref):
    near = part_ref.shape[0] // cores
    tails = tails_of(p_ref[:, members * MAIN :, :], members)
    for member in range(members):
        piece = rows_of(p_ref, tails, member, 1, members)
        part = lax.dot_general(piece, hid_ref[member], FIRST, preferred_element_type=F32)
        part = part.astype(BF16).reshape(near, cores, *part_ref.shape[2:])
        for c in range(cores):
            part_ref[c * near : (c + 1) * near, member] = part[:, c]


def input_kernel(members, x_hbm, p_hbm, tail_hbm, w_hbm, out_ref, *scratch):
    x_ref, p_ref, tail_ref, gate_ref, up_ref, down_ref, sems = scratch
    devs, _, width = out_ref.shape
    copies = fetch(
        sems,
        [(p_hbm, p_ref), (x_hbm, x_ref), (tail_hbm, tail_ref)]
        + parts_of(w_hbm, 0, gate_ref)
        + parts_of(w_hbm, 1, up_ref)
        + parts_of(w_hbm, 2, down_ref),
    )
    copies[0].wait()
    extra = tails_of(p_ref[:, members * MAIN :, :], members)
    for copy in copies[1:]:
        copy.wait()
    tails = [tail_ref[...]]
    for member in range(members):
        rows = rows_of(x_ref, extra, member, 0, members)
        piece = rows_of(p_ref, extra, member, 1, members)
        gate_w, up_w = matrix(gate_ref, member), matrix(up_ref, member)
        pre_gate = jnp.dot(rows, gate_w, preferred_element_type=F32)
        pre_up = jnp.dot(rows, up_w, preferred_element_type=F32)
        squash = 1.0 / (1.0 + jnp.exp(-pre_gate))
        hidden_grad = jnp.dot(piece, matrix(down_ref, member), preferred_element_type=F32)
        gate_pre = hidden_grad * pre_up * squash * (1.0 + pre_gate * (1.0 - squash))
        up_pre = hidden_grad * (pre_gate * squash)
        grad = (
            lax.dot_general(gate_pre.astype(BF16), gate_w, LAST, preferred_element_type=F32)
            + lax.dot_general(up_pre.astype(BF16), up_w, LAST, preferred_element_type=F32)
        ).astype(BF16)
        out_ref[:, member * MAIN : (member + 1) * MAIN, :] = grad[: devs * MAIN].reshape(
            devs, MAIN, width
        )
        tails.append(grad[devs * MAIN :])
    tails = jnp.concatenate(tails, axis=0)
    out_ref[:, members * MAIN :, :] = (
        lax.dot_general(tail_order(devs, members), tails, FIRST, preferred_element_type=F32)
        .astype(BF16)
        .reshape(devs, TAIL, width)
    )


def split(values):
    high = values.astype(BF16)
    return high, (values - high.astype(F32)).astype(BF16)


def gather(weights, rows):
    return lax.dot_general(weights, rows, FIRST, preferred_element_type=F32)


def first_combine(
    halves, cores, members, routes_ref, gates_ref, grad_ref, out_ref, mix_ref, gg_ref, hot_ref
):
    devs, side, width = out_ref.shape
    routes_t, gates_t = routes_ref[...], gates_ref[...]
    expert, slot = main_rows(grad_ref.shape[0], devs, halves, cores, members)
    chosen, gate = picks(routes_t, gates_t, expert, slot, True)
    hot_ref[...] = chosen.astype(F32).astype(BF16)
    out = out_ref[...].reshape(devs * side, width)
    high, low = split(gate)
    mix_ref[...] = gather(high, out) + gather(low, out)
    score = lax.dot_general(out, grad_ref[...], LAST, preferred_element_type=F32)
    score = jnp.where(chosen, score, 0.0)
    for k in range(routes_t.shape[0]):
        gg_ref[k : k + 1, :] = jnp.sum(
            jnp.where(expert == routes_t[k : k + 1, :], score, 0.0), axis=0, keepdims=True
        )


def last_combine(halves, cores, members, routes_ref, gates_ref, grad_ref, *refs):
    part_mix_ref, part_gg_ref, hot_ref, back_ref, mix_ref, in_ref, gg_ref = refs
    devs, rows, width = back_ref.shape
    side = rows - TAIL
    routes_t, gates_t = routes_ref[...], gates_ref[...]
    expert, kind = tail_rows(grad_ref.shape[0], devs, halves, cores, members)
    chosen, gate = picks(routes_t, gates_t, expert, MAIN, kind < 2)
    hot = jnp.where(kind == 1, chosen.astype(F32), 0.0).astype(BF16)
    chosen = chosen & (kind == 0)
    high, low = split(jnp.where(kind == 0, gate, 0.0))
    back = back_ref[:, :side, :].reshape(devs * side, width)
    tail = back_ref[:, side:, :].reshape(devs * TAIL, width)
    mix_ref[...] = (part_mix_ref[...] + gather(high, tail) + gather(low, tail)).astype(BF16)
    in_ref[...] = (gather(hot_ref[...], back) + gather(hot, tail)).astype(BF16)
    score = lax.dot_general(tail, grad_ref[...], LAST, preferred_element_type=F32)
    score = jnp.where(chosen, score, 0.0)
    for k in range(routes_t.shape[0]):
        gg_ref[k : k + 1, :] = part_gg_ref[k : k + 1, :] + jnp.sum(
            jnp.where(expert == routes_t[k : k + 1, :], score, 0.0), axis=0, keepdims=True
        )


def call(kernel, name, outs, flops, args, anywhere=(), scratch=(), room=60):
    flat = outs if isinstance(outs, tuple) else (outs,)
    total = sum(a.size * a.dtype.itemsize for a in (*args, *flat))
    inner = pl.BlockSpec()
    outer = pl.BlockSpec(memory_space=pltpu.HBM)
    return pl.pallas_call(
        kernel,
        name=name,
        out_shape=outs,
        in_specs=[outer if i in anywhere else inner for i in range(len(args))],
        out_specs=tuple(inner for _ in flat) if isinstance(outs, tuple) else inner,
        scratch_shapes=scratch,
        compiler_params=pltpu.CompilerParams(vmem_limit_bytes=room << 20),
        cost_estimate=pl.CostEstimate(flops=flops, bytes_accessed=total, transcendentals=0),
    )(*args)


def per_device(tokens, routes, gates, out_grad, w_gate, w_up, w_down):
    devs = lax.axis_size(PLANE)
    dp_devs = lax.axis_size(DP)
    halves = lax.axis_size("xh")
    cores = lax.axis_size("c")
    toks, width = tokens.shape
    members, slice_rows, units = w_gate.shape
    side = members * MAIN
    slots = devs * (MAIN + 1)
    shape = jax.ShapeDtypeStruct
    vmem = pltpu.VMEM
    dma = pltpu.SemaphoreType.DMA

    near = dp_devs // cores

    def order(cell):
        return cell % cores * near + cell // cores

    there = [
        (cell * dp_devs + order(other), other * dp_devs + order(cell))
        for cell in range(dp_devs)
        for other in range(dp_devs)
    ]

    with jax.named_scope("weights"):
        packed = jnp.stack([w_gate, w_up, w_down.transpose(0, 2, 1)])
        packed = lax.ppermute(packed, DP + ("z",), there)

    with jax.named_scope("send"):
        routes_t, gates_t = routes.T, gates.T
        send_x, send_p = call(
            functools.partial(send_kernel, halves, cores, members),
            "send",
            (shape((devs, side, width), BF16), shape((devs, side + TAIL, width), BF16)),
            4 * slots * members * toks * width,
            (routes_t, gates_t, tokens, out_grad),
        )
        packed, send_x = lax.optimization_barrier((packed, send_x))
        full = lax.all_gather(packed, "z", axis=0)
        weight = (full.shape[0], members, slice_rows, units)
        recv_x = swap(send_x, PLANE)
        send_p, recv_x = lax.optimization_barrier((send_p, recv_x))
        recv_p = swap(send_p, PLANE)

    unit = 2 * slots * members * width * units
    held = [vmem((near, cores, members, slice_rows, units), BF16)] * 3
    rows_x, rows_p = vmem(recv_x.shape, BF16), vmem(recv_p.shape, BF16)
    extra = vmem((devs, TAIL, width), BF16)
    with jax.named_scope("forward"):
        out, tail, hidden = call(
            functools.partial(forward_kernel, members),
            "forward",
            (
                shape((devs, side, width), BF16),
                shape((members * devs, width), BF16),
                shape((members, slots, units), BF16),
            ),
            3 * unit,
            (recv_x, recv_p, full),
            (0, 1, 2),
            (extra, rows_x, *held, dma((2 + 3 * cores,))),
        )
        back_out = swap(out, PLANE)

    with jax.named_scope("down_grad"):
        part = call(
            functools.partial(part_kernel, members, cores),
            "part",
            shape(weight, BF16),
            unit,
            (recv_p, hidden),
        )
        part = lax.psum_scatter(part, "z", scatter_dimension=0)

    with jax.named_scope("input_grad"):
        grad = call(
            functools.partial(input_kernel, members),
            "input_grad",
            shape((devs, side + TAIL, width), BF16),
            5 * unit,
            (recv_x, recv_p, tail, full),
            (0, 1, 2, 3),
            (rows_x, rows_p, vmem(tail.shape, BF16), *held, dma((3 + 3 * cores,))),
        )
        grad, back_out = lax.optimization_barrier((grad, back_out))
        back_grad = swap(grad, PLANE)

    with jax.named_scope("combine"):
        mix, gg, hot = call(
            functools.partial(first_combine, halves, cores, members),
            "first",
            (
                shape((toks, width), F32),
                shape(routes_t.shape, F32),
                shape((devs * side, toks), BF16),
            ),
            6 * devs * side * toks * width,
            (routes_t, gates_t, out_grad, back_out),
            room=24,
        )
        part, back_grad, mix = lax.optimization_barrier((part, back_grad, mix))
        mixed, input_grad, gate_grad = call(
            functools.partial(last_combine, halves, cores, members),
            "last",
            (
                shape((toks, width), BF16),
                shape((toks, width), BF16),
                shape(routes_t.shape, F32),
            ),
            4 * devs * side * toks * width,
            (routes_t, gates_t, out_grad, mix, gg, hot, back_grad),
            room=24,
        )

    with jax.named_scope("down_grad"):
        part = lax.ppermute(part, DP + ("z",), there)
        down_grad = part.transpose(0, 2, 1).astype(F32)
    return (mixed, input_grad, gate_grad.T, down_grad)


def solution(mesh):
    fine = Mesh(mesh.devices.reshape(2, 4, 2, 2, 16), BLOCKS)
    rows = P(BLOCKS, None)
    return jax.shard_map(
        per_device,
        mesh=fine,
        in_specs=(
            rows,
            rows,
            rows,
            rows,
            P(("xh", "z"), DP, None),
            P(("xh", "z"), DP, None),
            P(("xh", "z"), None, DP),
        ),
        out_specs=(rows, rows, rows, P(("xh", "z"), None, DP)),
        check_vma=False,
    )
```

```python
import functools

import jax
import jax.numpy as jnp
from jax import lax
from jax.experimental import pallas as pl
from jax.experimental.pallas import tpu as pltpu
from jax.sharding import Mesh, PartitionSpec as P

DP = ("xl", "y", "c")
PLANE = ("xl", "y", "c", "xh")
BLOCKS = ("xl", "y", "c", "xh", "z")

MAIN = 16
TAIL = 8
F32 = jnp.float32
BF16 = jnp.bfloat16
LAST = (((1,), (1,)), ((), ()))
FIRST = (((0,), (0,)), ((), ()))


def swap(values, axes):
    return lax.all_to_all(values, axes, split_axis=0, concat_axis=0, tiled=True)


def picks(routes_t, gates_t, expert, slot, allowed):
    rows, toks = expert.shape
    match = jnp.zeros((rows, toks), F32)
    gate = jnp.zeros((rows, toks), F32)
    for k in range(routes_t.shape[0]):
        hit = expert == routes_t[k : k + 1, :]
        match = jnp.where(hit, 1.0, match)
        gate = jnp.where(hit, gates_t[k : k + 1, :], gate)
    before = lax.broadcasted_iota(jnp.int32, (toks, toks), 0) < lax.broadcasted_iota(
        jnp.int32, (toks, toks), 1
    )
    rank = jnp.dot(match.astype(BF16), before.astype(BF16), preferred_element_type=F32)
    chosen = (match > 0.5) & (rank.astype(jnp.int32) == slot) & allowed
    return chosen, jnp.where(chosen, gate, 0.0)


def expert_of(dev, member, devs, halves, cores, members):
    cell = dev // halves
    depth = devs // halves
    pair = dev % halves * depth + cell % cores * (depth // cores) + cell // cores
    return pair * members + member


def main_rows(member, toks, devs, halves, cores, members):
    row = lax.broadcasted_iota(jnp.int32, (devs * MAIN, toks), 0)
    return expert_of(row // MAIN, member, devs, halves, cores, members), row % MAIN


def tail_rows(toks, devs, halves, cores, members):
    row = lax.broadcasted_iota(jnp.int32, (devs * TAIL, toks), 0)
    dev, place = row // TAIL, row % TAIL
    return expert_of(dev, place % members, devs, halves, cores, members), place // members


def pack_kernel(gate_ref, up_ref, down_ref, *packed):
    for member, ref in enumerate(packed):
        for which, weight in enumerate((gate_ref, up_ref, down_ref)):
            ref[which] = weight[member]


def send_kernel(halves, cores, members, routes_ref, gates_ref, tok_ref, grad_ref, send_ref):
    devs, _, width = send_ref.shape
    toks = tok_ref.shape[0]
    routes_t, gates_t = routes_ref[...], gates_ref[...]
    tok, grad = tok_ref[...], grad_ref[...]
    for member in range(members):
        expert, slot = main_rows(member, toks, devs, halves, cores, members)
        chosen, gate = picks(routes_t, gates_t, expert, slot, True)
        hot = chosen.astype(F32).astype(BF16)
        put(send_ref, member, jnp.dot(hot, tok, preferred_element_type=F32).astype(BF16))
        scale = jnp.sum(gate, axis=1, keepdims=True)
        rows = scale * jnp.dot(hot, grad, preferred_element_type=F32)
        put(send_ref, members + member, rows.astype(BF16))
    expert, kind = tail_rows(toks, devs, halves, cores, members)
    chosen, gate = picks(routes_t, gates_t, expert, MAIN, kind < 2)
    hot = chosen.astype(F32)
    scale = jnp.sum(gate, axis=1, keepdims=True)
    hot_x = jnp.where(kind == 0, hot, 0.0).astype(BF16)
    hot_p = jnp.where(kind == 1, hot, 0.0).astype(BF16)
    rows = jnp.dot(hot_x, tok, preferred_element_type=F32) + scale * jnp.dot(
        hot_p, grad, preferred_element_type=F32
    )
    put_tail(send_ref, rows.astype(BF16))


def put(ref, place, rows):
    ref[:, place * MAIN : (place + 1) * MAIN, :] = rows.reshape(-1, MAIN, rows.shape[-1])


def put_tail(ref, rows):
    ref[:, ref.shape[1] - TAIL :, :] = rows.reshape(-1, TAIL, rows.shape[-1])


def take(ref, place):
    return ref[:, place * MAIN : (place + 1) * MAIN, :].reshape(-1, ref.shape[-1])


def take_tail(ref):
    return ref[:, ref.shape[1] - TAIL :, :].reshape(-1, ref.shape[-1])


def tail_order(devs, members):
    shape = (2 * members * devs, devs * TAIL)
    row = lax.broadcasted_iota(jnp.int32, shape, 0)
    col = lax.broadcasted_iota(jnp.int32, shape, 1)
    return (col == row % devs * TAIL + row // devs).astype(F32).astype(BF16)


def tails_of(ref, members):
    order = tail_order(ref.shape[0], members)
    return jnp.dot(order, take_tail(ref), preferred_element_type=F32).astype(BF16)


def rows_of(ref, tails, place):
    devs = ref.shape[0]
    return jnp.concatenate([take(ref, place), tails[place * devs : (place + 1) * devs]], axis=0)


def fetch(sems, pairs):
    copies = [pltpu.make_async_copy(src, dst, sems.at[i]) for i, (src, dst) in enumerate(pairs)]
    for copy in copies:
        copy.start()
    return copies


def pieces(depth, cores, shift):
    near = depth // cores
    found = []
    for c in range(cores):
        at = (c * near + shift) % depth
        count = min(near, depth - at)
        found.append((c, 0, at, count))
        if count < near:
            found.append((c, count, 0, near - count))
    return found


def parts_of(w_hbm, shifts, which, ref):
    return [
        (
            w_hbm.at[at : at + count, member, which],
            ref.at[cell : cell + count, c, member],
        )
        for member, shift in enumerate(shifts)
        for c, cell, at, count in pieces(w_hbm.shape[0], ref.shape[1], shift)
    ]


def matrix(ref, member):
    near, cores, _, rows, units = ref.shape
    return ref[:, :, member].reshape(near * cores * rows, units)


def forward_kernel(shifts, rows_hbm, w_hbm, out_ref, tail_ref, part_ref, *scratch):
    rows_ref, gate_ref, up_ref, down_ref, sems = scratch
    members = len(shifts)
    near, cores = gate_ref.shape[:2]
    devs = rows_ref.shape[0]
    copies = fetch(
        sems,
        [(rows_hbm, rows_ref)]
        + parts_of(w_hbm, shifts, 0, gate_ref)
        + parts_of(w_hbm, shifts, 1, up_ref)
        + parts_of(w_hbm, shifts, 2, down_ref),
    )
    copies[0].wait()
    tails = tails_of(rows_ref, members)
    for copy in copies[1:]:
        copy.wait()
    for member in range(members):
        rows = rows_of(rows_ref, tails, member)
        piece = rows_of(rows_ref, tails, members + member)
        pre_gate = jnp.dot(rows, matrix(gate_ref, member), preferred_element_type=F32)
        pre_up = jnp.dot(rows, matrix(up_ref, member), preferred_element_type=F32)
        active = pre_gate / (1.0 + jnp.exp(-pre_gate))
        hidden = (active * pre_up).astype(BF16)
        out = lax.dot_general(hidden, matrix(down_ref, member), LAST, preferred_element_type=F32)
        out = out.astype(BF16)
        put(out_ref, member, out[: devs * MAIN])
        tail_ref[member * devs : (member + 1) * devs] = out[devs * MAIN :]
        part = lax.dot_general(piece, hidden, FIRST, preferred_element_type=F32)
        part = part.astype(BF16).reshape(near, cores, *part_ref.shape[2:])
        for c in range(cores):
            part_ref[c * near : (c + 1) * near, member] = part[:, c]


def input_kernel(shifts, rows_hbm, tail_hbm, w_hbm, out_ref, *scratch):
    rows_ref, tail_ref, gate_ref, up_ref, down_ref, sems = scratch
    members = len(shifts)
    devs = rows_ref.shape[0]
    copies = fetch(
        sems,
        [(rows_hbm, rows_ref), (tail_hbm, tail_ref)]
        + parts_of(w_hbm, shifts, 0, gate_ref)
        + parts_of(w_hbm, shifts, 1, up_ref)
        + parts_of(w_hbm, shifts, 2, down_ref),
    )
    copies[0].wait()
    extra = tails_of(rows_ref, members)
    for copy in copies[1:]:
        copy.wait()
    tails = [tail_ref[...]]
    for member in range(members):
        given = rows_of(rows_ref, extra, member)
        piece = rows_of(rows_ref, extra, members + member)
        gate_w, up_w = matrix(gate_ref, member), matrix(up_ref, member)
        pre_gate = jnp.dot(given, gate_w, preferred_element_type=F32)
        pre_up = jnp.dot(given, up_w, preferred_element_type=F32)
        squash = 1.0 / (1.0 + jnp.exp(-pre_gate))
        hidden_grad = jnp.dot(piece, matrix(down_ref, member), preferred_element_type=F32)
        gate_pre = hidden_grad * pre_up * squash * (1.0 + pre_gate * (1.0 - squash))
        up_pre = hidden_grad * (pre_gate * squash)
        grad = (
            lax.dot_general(gate_pre.astype(BF16), gate_w, LAST, preferred_element_type=F32)
            + lax.dot_general(up_pre.astype(BF16), up_w, LAST, preferred_element_type=F32)
        ).astype(BF16)
        put(out_ref, member, grad[: devs * MAIN])
        tails.append(grad[devs * MAIN :])
    tails = jnp.concatenate(tails, axis=0)
    tails = lax.dot_general(tail_order(devs, members), tails, FIRST, preferred_element_type=F32)
    put_tail(out_ref, tails.astype(BF16))


def split(values):
    high = values.astype(BF16)
    return high, (values - high.astype(F32)).astype(BF16)


def gather(weights, rows):
    return lax.dot_general(weights, rows, FIRST, preferred_element_type=F32)


def by_choice(routes_t, expert, score):
    return [
        jnp.sum(jnp.where(expert == routes_t[k : k + 1, :], score, 0.0), axis=0, keepdims=True)
        for k in range(routes_t.shape[0])
    ]


def scores(chosen, rows, og):
    return jnp.where(chosen, lax.dot_general(rows, og, LAST, preferred_element_type=F32), 0.0)


def first_combine(halves, cores, members, routes_ref, gates_ref, grad_ref, out_ref, *outs):
    mix_ref, gg_ref, hot_ref = outs
    devs = out_ref.shape[0]
    routes_t, gates_t, og = routes_ref[...], gates_ref[...], grad_ref[...]
    mix, lines = 0.0, [0.0] * routes_t.shape[0]
    for member in range(members):
        expert, slot = main_rows(member, og.shape[0], devs, halves, cores, members)
        chosen, gate = picks(routes_t, gates_t, expert, slot, True)
        hot_ref[member] = chosen.astype(F32).astype(BF16)
        high, low = split(gate)
        out = take(out_ref, member)
        mix = mix + gather(high, out) + gather(low, out)
        more = by_choice(routes_t, expert, scores(chosen, out, og))
        lines = [a + b for a, b in zip(lines, more)]
    mix_ref[...] = mix
    for k, line in enumerate(lines):
        gg_ref[k : k + 1, :] = line


def last_combine(halves, cores, members, routes_ref, gates_ref, grad_ref, *refs):
    part_mix_ref, part_gg_ref, hot_ref, back_ref, mix_ref, in_ref, gg_ref = refs
    routes_t, gates_t, og = routes_ref[...], gates_ref[...], grad_ref[...]
    expert, kind = tail_rows(og.shape[0], back_ref.shape[0], halves, cores, members)
    chosen, gate = picks(routes_t, gates_t, expert, MAIN, kind < 2)
    hot = jnp.where(kind == 1, chosen.astype(F32), 0.0).astype(BF16)
    chosen = chosen & (kind == 0)
    high, low = split(jnp.where(kind == 0, gate, 0.0))
    tail = take_tail(back_ref)
    mix_ref[...] = (part_mix_ref[...] + gather(high, tail) + gather(low, tail)).astype(BF16)
    summed = gather(hot, tail)
    for member in range(members):
        summed = summed + gather(hot_ref[member], take(back_ref, member))
    in_ref[...] = summed.astype(BF16)
    for k, line in enumerate(by_choice(routes_t, expert, scores(chosen, tail, og))):
        gg_ref[k : k + 1, :] = part_gg_ref[k : k + 1, :] + line


def call(kernel, name, outs, flops, args, anywhere=(), scratch=(), room=60):
    flat = outs if isinstance(outs, tuple) else (outs,)
    total = sum(a.size * a.dtype.itemsize for a in (*args, *flat))
    inner = pl.BlockSpec()
    outer = pl.BlockSpec(memory_space=pltpu.HBM)
    return pl.pallas_call(
        kernel,
        name=name,
        out_shape=outs,
        in_specs=[outer if i in anywhere else inner for i in range(len(args))],
        out_specs=tuple(inner for _ in flat) if isinstance(outs, tuple) else inner,
        scratch_shapes=scratch,
        compiler_params=pltpu.CompilerParams(vmem_limit_bytes=room << 20),
        cost_estimate=pl.CostEstimate(flops=flops, bytes_accessed=total, transcendentals=0),
    )(*args)


def per_device(tokens, routes, gates, out_grad, w_gate, w_up, w_down):
    devs = lax.axis_size(PLANE)
    dp_devs = lax.axis_size(DP)
    halves = lax.axis_size("xh")
    cores = lax.axis_size("c")
    depth = lax.axis_size("z")
    toks, width = tokens.shape
    members, slice_rows, units = w_gate.shape
    side = members * MAIN
    slots = devs * (MAIN + 1)
    shape = jax.ShapeDtypeStruct
    vmem = pltpu.VMEM
    dma = pltpu.SemaphoreType.DMA
    near = dp_devs // cores

    def order(cell):
        return cell % cores * near + cell // cores

    def moves(shift):
        return [
            (cell * depth + order(other), other * depth + (order(cell) + shift) % depth)
            for cell in range(dp_devs)
            for other in range(dp_devs)
        ]

    shifts = [member * (depth // 4) for member in range(members)]
    axes = DP + ("z",)

    with jax.named_scope("weights"):
        each = shape((3, slice_rows, units), BF16)
        packed = call(
            pack_kernel, "pack", (each,) * members, 0, (w_gate, w_up, w_down.transpose(0, 2, 1))
        )
        packed = [lax.ppermute(w, axes, moves(shift)) for w, shift in zip(packed, shifts)]
        packed = jnp.stack(packed)

    with jax.named_scope("send"):
        routes_t, gates_t = routes.T, gates.T
        rows = call(
            functools.partial(send_kernel, halves, cores, members),
            "send",
            shape((devs, 2 * side + TAIL, width), BF16),
            4 * slots * members * toks * width,
            (routes_t, gates_t, tokens, out_grad),
        )
        packed, rows = lax.optimization_barrier((packed, rows))
        full = lax.all_gather(packed, "z", axis=0)
        rows = swap(rows, PLANE)

    unit = 2 * slots * members * width * units
    held = [vmem((near, cores, members, slice_rows, units), BF16)] * 3
    count = 3 * sum(len(pieces(depth, cores, shift)) for shift in shifts)
    with jax.named_scope("forward"):
        out, tail, part = call(
            functools.partial(forward_kernel, shifts),
            "forward",
            (
                shape((devs, side, width), BF16),
                shape((members * devs, width), BF16),
                shape((depth, members, slice_rows, units), BF16),
            ),
            4 * unit,
            (rows, full),
            (0, 1),
            (vmem(rows.shape, BF16), *held, dma((1 + count,))),
        )
        back_out = swap(out, PLANE)

    with jax.named_scope("down_grad"):
        part = lax.psum_scatter(part, "z", scatter_dimension=0)

    with jax.named_scope("input_grad"):
        grad = call(
            functools.partial(input_kernel, shifts),
            "input_grad",
            shape((devs, side + TAIL, width), BF16),
            5 * unit,
            (rows, tail, full),
            (0, 1, 2),
            (vmem(rows.shape, BF16), vmem(tail.shape, BF16), *held, dma((2 + count,))),
        )
        grad, back_out = lax.optimization_barrier((grad, back_out))
        back_grad = swap(grad, PLANE)

    with jax.named_scope("combine"):
        lines = shape(routes_t.shape, F32)
        mix, gg, hot = call(
            functools.partial(first_combine, halves, cores, members),
            "first",
            (
                shape((toks, width), F32),
                lines,
                shape((members, devs * MAIN, toks), BF16),
            ),
            6 * devs * side * toks * width,
            (routes_t, gates_t, out_grad, back_out),
            room=24,
        )
        part, back_grad, mix = lax.optimization_barrier((part, back_grad, mix))
        mixed, input_grad, gate_grad = call(
            functools.partial(last_combine, halves, cores, members),
            "last",
            (shape((toks, width), BF16), shape((toks, width), BF16), lines),
            4 * devs * side * toks * width,
            (routes_t, gates_t, out_grad, mix, gg, hot, back_grad),
            room=24,
        )

    with jax.named_scope("down_grad"):
        part = lax.ppermute(part, axes, moves(0))
        down_grad = part.transpose(0, 2, 1).astype(F32)
    return (mixed, input_grad, gate_grad.T, down_grad)


def solution(mesh):
    fine = Mesh(mesh.devices.reshape(2, 4, 2, 2, 16), BLOCKS)
    rows = P(BLOCKS, None)
    return jax.shard_map(
        per_device,
        mesh=fine,
        in_specs=(
            rows,
            rows,
            rows,
            rows,
            P(("xh", "z"), DP, None),
            P(("xh", "z"), DP, None),
            P(("xh", "z"), None, DP),
        ),
        out_specs=(rows, rows, rows, P(("xh", "z"), None, DP)),
        check_vma=False,
    )
```

```python
import functools

import jax
import jax.numpy as jnp
from jax import lax
from jax.experimental import pallas as pl
from jax.experimental.pallas import tpu as pltpu
from jax.sharding import Mesh, PartitionSpec as P

DP = ("xl", "y", "c")
PLANE = ("xl", "y", "c", "xh")
BLOCKS = ("xl", "y", "c", "xh", "z")

MAIN = 16
TAIL = 8
F32 = jnp.float32
BF16 = jnp.bfloat16
LAST = (((1,), (1,)), ((), ()))
FIRST = (((0,), (0,)), ((), ()))


def swap(values, axes):
    return lax.all_to_all(values, axes, split_axis=0, concat_axis=0, tiled=True)


def picks(routes_t, gates_t, expert, slot, allowed):
    rows, toks = expert.shape
    match = jnp.zeros((rows, toks), F32)
    gate = jnp.zeros((rows, toks), F32)
    for k in range(routes_t.shape[0]):
        hit = expert == routes_t[k : k + 1, :]
        match = jnp.where(hit, 1.0, match)
        gate = jnp.where(hit, gates_t[k : k + 1, :], gate)
    before = lax.broadcasted_iota(jnp.int32, (toks, toks), 0) < lax.broadcasted_iota(
        jnp.int32, (toks, toks), 1
    )
    rank = jnp.dot(match.astype(BF16), before.astype(BF16), preferred_element_type=F32)
    chosen = (match > 0.5) & (rank.astype(jnp.int32) == slot) & allowed
    return chosen, jnp.where(chosen, gate, 0.0)


def expert_of(dev, member, devs, halves, cores, members):
    cell = dev // halves
    depth = devs // halves
    pair = dev % halves * depth + cell % cores * (depth // cores) + cell // cores
    return pair * members + member


def main_rows(member, toks, devs, halves, cores, members):
    row = lax.broadcasted_iota(jnp.int32, (devs * MAIN, toks), 0)
    return expert_of(row // MAIN, member, devs, halves, cores, members), row % MAIN


def tail_rows(toks, devs, halves, cores, members):
    row = lax.broadcasted_iota(jnp.int32, (devs * TAIL, toks), 0)
    dev, place = row // TAIL, row % TAIL
    return expert_of(dev, place % members, devs, halves, cores, members), place // members


def pack_kernel(gate_ref, up_ref, down_ref, *packed):
    for member, ref in enumerate(packed):
        for which, weight in enumerate((gate_ref, up_ref, down_ref)):
            ref[which] = weight[member]


def send_kernel(halves, cores, members, routes_ref, gates_ref, tok_ref, grad_ref, *outs):
    send_ref, hot_ref, high_ref, low_ref, hot_tail_ref, high_tail_ref, low_tail_ref = outs
    devs, _, width = send_ref.shape
    toks = tok_ref.shape[0]
    routes_t, gates_t = routes_ref[...], gates_ref[...]
    tok, grad = tok_ref[...], grad_ref[...]
    for member in range(members):
        expert, slot = main_rows(member, toks, devs, halves, cores, members)
        chosen, gate = picks(routes_t, gates_t, expert, slot, True)
        hot = chosen.astype(F32).astype(BF16)
        put(send_ref, member, jnp.dot(hot, tok, preferred_element_type=F32).astype(BF16))
        scale = jnp.sum(gate, axis=1, keepdims=True)
        rows = scale * jnp.dot(hot, grad, preferred_element_type=F32)
        put(send_ref, members + member, rows.astype(BF16))
        hot_ref[member] = hot
        high_ref[member], low_ref[member] = split(gate)
    expert, kind = tail_rows(toks, devs, halves, cores, members)
    chosen, gate = picks(routes_t, gates_t, expert, MAIN, kind < 2)
    hot = chosen.astype(F32)
    scale = jnp.sum(gate, axis=1, keepdims=True)
    hot_x = jnp.where(kind == 0, hot, 0.0).astype(BF16)
    hot_p = jnp.where(kind == 1, hot, 0.0).astype(BF16)
    rows = jnp.dot(hot_x, tok, preferred_element_type=F32) + scale * jnp.dot(
        hot_p, grad, preferred_element_type=F32
    )
    put_tail(send_ref, rows.astype(BF16))
    hot_tail_ref[0], hot_tail_ref[1] = hot_x, hot_p
    high_tail_ref[...], low_tail_ref[...] = split(jnp.where(kind == 0, gate, 0.0))


def put(ref, place, rows):
    ref[:, place * MAIN : (place + 1) * MAIN, :] = rows.reshape(-1, MAIN, rows.shape[-1])


def put_tail(ref, rows):
    ref[:, ref.shape[1] - TAIL :, :] = rows.reshape(-1, TAIL, rows.shape[-1])


def take(ref, place):
    return ref[:, place * MAIN : (place + 1) * MAIN, :].reshape(-1, ref.shape[-1])


def take_tail(ref):
    return ref[:, ref.shape[1] - TAIL :, :].reshape(-1, ref.shape[-1])


def tail_order(devs, members):
    shape = (2 * members * devs, devs * TAIL)
    row = lax.broadcasted_iota(jnp.int32, shape, 0)
    col = lax.broadcasted_iota(jnp.int32, shape, 1)
    return (col == row % devs * TAIL + row // devs).astype(F32).astype(BF16)


def tails_of(ref, members):
    order = tail_order(ref.shape[0], members)
    return jnp.dot(order, take_tail(ref), preferred_element_type=F32).astype(BF16)


def rows_of(ref, tails, place):
    devs = ref.shape[0]
    return jnp.concatenate([take(ref, place), tails[place * devs : (place + 1) * devs]], axis=0)


def fetch(sems, pairs):
    copies = [pltpu.make_async_copy(src, dst, sems.at[i]) for i, (src, dst) in enumerate(pairs)]
    for copy in copies:
        copy.start()
    return copies


def pieces(depth, cores, shift):
    near = depth // cores
    found = []
    for c in range(cores):
        at = (c * near + shift) % depth
        count = min(near, depth - at)
        found.append((c, 0, at, count))
        if count < near:
            found.append((c, count, 0, near - count))
    return found


def parts_of(w_hbm, member, shift, which, ref):
    return [
        (w_hbm.at[at : at + count, member, which], ref.at[cell : cell + count, c, member])
        for c, cell, at, count in pieces(w_hbm.shape[0], ref.shape[1], shift)
    ]


def matrix(ref, member):
    near, cores, _, rows, units = ref.shape
    return ref[:, :, member].reshape(near * cores * rows, units)


def arrive(sems, rows_hbm, rows_ref, w_hbm, shifts, matrices):
    members = len(shifts)
    pairs, groups = [(rows_hbm, rows_ref)], []
    for member in range(members):
        found = [
            pair
            for which, ref in matrices
            for pair in parts_of(w_hbm, member, shifts[member], which, ref)
        ]
        groups.append(slice(len(pairs), len(pairs) + len(found)))
        pairs += found
    copies = fetch(sems, pairs)

    def wait(member):
        for copy in copies[groups[member]]:
            copy.wait()

    return copies[0].wait, wait


def hidden_kernel(shifts, rows_hbm, w_hbm, part_ref, rows_ref, gate_ref, up_ref, sems):
    members = len(shifts)
    near, cores = gate_ref.shape[:2]
    rows_here, weights_here = arrive(
        sems, rows_hbm, rows_ref, w_hbm, shifts, ((0, gate_ref), (1, up_ref))
    )
    rows_here()
    tails = tails_of(rows_ref, members)
    for member in range(members):
        rows = rows_of(rows_ref, tails, member)
        piece = rows_of(rows_ref, tails, members + member)
        weights_here(member)
        pre_gate = jnp.dot(rows, matrix(gate_ref, member), preferred_element_type=F32)
        pre_up = jnp.dot(rows, matrix(up_ref, member), preferred_element_type=F32)
        active = pre_gate / (1.0 + jnp.exp(-pre_gate))
        hidden = (active * pre_up).astype(BF16)
        part = lax.dot_general(piece, hidden, FIRST, preferred_element_type=F32)
        part = part.reshape(near, cores, *part_ref.shape[2:])
        for c in range(cores):
            part_ref[c * near : (c + 1) * near, member] = part[:, c]


def rest_kernel(shifts, rows_hbm, w_hbm, back_ref, rows_ref, gate_ref, up_ref, down_ref, sems):
    members = len(shifts)
    devs = rows_ref.shape[0]
    rows_here, weights_here = arrive(
        sems, rows_hbm, rows_ref, w_hbm, shifts, ((0, gate_ref), (1, up_ref), (2, down_ref))
    )
    rows_here()
    extra = tails_of(rows_ref, members)
    tails = [None] * (2 * members)
    for member in range(members):
        rows = rows_of(rows_ref, extra, member)
        piece = rows_of(rows_ref, extra, members + member)
        weights_here(member)
        gate_w, up_w, down_w = (matrix(ref, member) for ref in (gate_ref, up_ref, down_ref))
        pre_gate = jnp.dot(rows, gate_w, preferred_element_type=F32)
        pre_up = jnp.dot(rows, up_w, preferred_element_type=F32)
        squash = 1.0 / (1.0 + jnp.exp(-pre_gate))
        active = pre_gate * squash
        hidden = (active * pre_up).astype(BF16)
        out = lax.dot_general(hidden, down_w, LAST, preferred_element_type=F32).astype(BF16)
        put(back_ref, member, out[: devs * MAIN])
        tails[member] = out[devs * MAIN :]
        hidden_grad = jnp.dot(piece, down_w, preferred_element_type=F32)
        gate_pre = hidden_grad * pre_up * squash * (1.0 + pre_gate * (1.0 - squash))
        up_pre = hidden_grad * active
        grad = (
            lax.dot_general(gate_pre.astype(BF16), gate_w, LAST, preferred_element_type=F32)
            + lax.dot_general(up_pre.astype(BF16), up_w, LAST, preferred_element_type=F32)
        ).astype(BF16)
        put(back_ref, members + member, grad[: devs * MAIN])
        tails[members + member] = grad[devs * MAIN :]
    tails = jnp.concatenate(tails, axis=0)
    tails = lax.dot_general(tail_order(devs, members), tails, FIRST, preferred_element_type=F32)
    put_tail(back_ref, tails.astype(BF16))


def split(values):
    high = values.astype(BF16)
    return high, (values - high.astype(F32)).astype(BF16)


def gather(weights, rows):
    return lax.dot_general(weights, rows, FIRST, preferred_element_type=F32)


def by_choice(routes_t, expert, score):
    return [
        jnp.sum(jnp.where(expert == routes_t[k : k + 1, :], score, 0.0), axis=0, keepdims=True)
        for k in range(routes_t.shape[0])
    ]


def scores(chosen, rows, og):
    return jnp.where(chosen, lax.dot_general(rows, og, LAST, preferred_element_type=F32), 0.0)


def combine_kernel(halves, cores, members, routes_ref, grad_ref, *refs):
    hot_ref, high_ref, low_ref, hot_tail_ref, high_tail_ref, low_tail_ref = refs[:6]
    back_ref, mix_ref, in_ref, gg_ref = refs[6:]
    devs = back_ref.shape[0]
    routes_t, og = routes_ref[...], grad_ref[...]
    toks = og.shape[0]
    tail = take_tail(back_ref)
    expert, _ = tail_rows(toks, devs, halves, cores, members)
    lines = by_choice(routes_t, expert, scores(hot_tail_ref[0].astype(F32) > 0.5, tail, og))
    mix = gather(high_tail_ref[...], tail) + gather(low_tail_ref[...], tail)
    summed = gather(hot_tail_ref[1], tail)
    for member in range(members):
        out = take(back_ref, member)
        mix = mix + gather(high_ref[member], out) + gather(low_ref[member], out)
        summed = summed + gather(hot_ref[member], take(back_ref, members + member))
        expert, _ = main_rows(member, toks, devs, halves, cores, members)
        chosen = hot_ref[member].astype(F32) > 0.5
        more = by_choice(routes_t, expert, scores(chosen, out, og))
        lines = [a + b for a, b in zip(lines, more)]
    mix_ref[...] = mix.astype(BF16)
    in_ref[...] = summed.astype(BF16)
    for k, line in enumerate(lines):
        gg_ref[k : k + 1, :] = line


def call(kernel, name, outs, flops, args, anywhere=(), scratch=(), room=60):
    flat = outs if isinstance(outs, tuple) else (outs,)
    total = sum(a.size * a.dtype.itemsize for a in (*args, *flat))
    inner = pl.BlockSpec()
    outer = pl.BlockSpec(memory_space=pltpu.HBM)
    return pl.pallas_call(
        kernel,
        name=name,
        out_shape=outs,
        in_specs=[outer if i in anywhere else inner for i in range(len(args))],
        out_specs=tuple(inner for _ in flat) if isinstance(outs, tuple) else inner,
        scratch_shapes=scratch,
        compiler_params=pltpu.CompilerParams(vmem_limit_bytes=room << 20),
        cost_estimate=pl.CostEstimate(flops=flops, bytes_accessed=total, transcendentals=0),
    )(*args)


def per_device(tokens, routes, gates, out_grad, w_gate, w_up, w_down):
    devs = lax.axis_size(PLANE)
    dp_devs = lax.axis_size(DP)
    halves = lax.axis_size("xh")
    cores = lax.axis_size("c")
    depth = lax.axis_size("z")
    toks, width = tokens.shape
    members, slice_rows, units = w_gate.shape
    side = members * MAIN
    slots = devs * (MAIN + 1)
    shape = jax.ShapeDtypeStruct
    vmem = pltpu.VMEM
    dma = pltpu.SemaphoreType.DMA
    near = dp_devs // cores

    def order(cell):
        return cell % cores * near + cell // cores

    def moves(shift):
        return [
            (cell * depth + order(other), other * depth + (order(cell) + shift) % depth)
            for cell in range(dp_devs)
            for other in range(dp_devs)
        ]

    shifts = [member * (depth // 4) for member in range(members)]
    axes = DP + ("z",)

    with jax.named_scope("weights"):
        each = shape((3, slice_rows, units), BF16)
        packed = call(
            pack_kernel, "pack", (each,) * members, 0, (w_gate, w_up, w_down.transpose(0, 2, 1))
        )
        packed = [lax.ppermute(w, axes, moves(shift)) for w, shift in zip(packed, shifts)]
        packed = jnp.stack(packed)

    with jax.named_scope("send"):
        routes_t, gates_t = routes.T, gates.T
        main = shape((members, devs * MAIN, toks), BF16)
        extra = shape((devs * TAIL, toks), BF16)
        rows, *who = call(
            functools.partial(send_kernel, halves, cores, members),
            "send",
            (
                shape((devs, 2 * side + TAIL, width), BF16),
                main,
                main,
                main,
                shape((2, devs * TAIL, toks), BF16),
                extra,
                extra,
            ),
            4 * slots * members * toks * width,
            (routes_t, gates_t, tokens, out_grad),
        )
        packed, rows = lax.optimization_barrier((packed, rows))
        full = lax.all_gather(packed, "z", axis=0)
        rows = swap(rows, PLANE)

    unit = 2 * slots * members * width * units
    held = vmem((near, cores, members, slice_rows, units), BF16)
    count = sum(len(pieces(depth, cores, shift)) for shift in shifts)
    with jax.named_scope("hidden"):
        part = call(
            functools.partial(hidden_kernel, shifts),
            "hidden",
            shape((depth, members, slice_rows, units), F32),
            3 * unit,
            (rows, full),
            (0, 1),
            (vmem(rows.shape, BF16), held, held, dma((1 + 2 * count,))),
        )
        rows, part = lax.optimization_barrier((rows, part))

    with jax.named_scope("down_grad"):
        part = lax.psum_scatter(part, "z", scatter_dimension=0)
        part = lax.ppermute(part.astype(BF16), axes, moves(0))

    with jax.named_scope("rest"):
        back = call(
            functools.partial(rest_kernel, shifts),
            "rest",
            shape(rows.shape, BF16),
            6 * unit,
            (rows, full),
            (0, 1),
            (vmem(rows.shape, BF16), held, held, held, dma((1 + 3 * count,))),
        )
        back = swap(back, PLANE)

    with jax.named_scope("combine"):
        mixed, input_grad, gate_grad = call(
            functools.partial(combine_kernel, halves, cores, members),
            "combine",
            (shape((toks, width), BF16), shape((toks, width), BF16), shape(routes_t.shape, F32)),
            8 * slots * members * toks * width,
            (routes_t, out_grad, *who, back),
            room=24,
        )

    with jax.named_scope("down_grad"):
        part, mixed = lax.optimization_barrier((part, mixed))
        down_grad = part.transpose(0, 2, 1).astype(F32)
    return (mixed, input_grad, gate_grad.T, down_grad)


def solution(mesh):
    fine = Mesh(mesh.devices.reshape(2, 4, 2, 2, 16), BLOCKS)
    rows = P(BLOCKS, None)
    return jax.shard_map(
        per_device,
        mesh=fine,
        in_specs=(
            rows,
            rows,
            rows,
            rows,
            P(("xh", "z"), DP, None),
            P(("xh", "z"), DP, None),
            P(("xh", "z"), None, DP),
        ),
        out_specs=(rows, rows, rows, P(("xh", "z"), None, DP)),
        check_vma=False,
    )
```

```python
import functools

import jax
import jax.numpy as jnp
from jax import lax
from jax.experimental import pallas as pl
from jax.experimental.pallas import tpu as pltpu
from jax.sharding import Mesh, PartitionSpec as P

DP = ("xl", "y", "c")
PLANE = ("xl", "y", "c", "xh")
BLOCKS = ("xl", "y", "c", "xh", "z")

MAIN = 16
TAIL = 8
F32 = jnp.float32
BF16 = jnp.bfloat16
LAST = (((1,), (1,)), ((), ()))
FIRST = (((0,), (0,)), ((), ()))


def swap(values, axes):
    return lax.all_to_all(values, axes, split_axis=0, concat_axis=0, tiled=True)


def picks(routes_t, gates_t, expert, slot, allowed):
    rows, toks = expert.shape
    match = jnp.zeros((rows, toks), F32)
    gate = jnp.zeros((rows, toks), F32)
    for k in range(routes_t.shape[0]):
        hit = expert == routes_t[k : k + 1, :]
        match = jnp.where(hit, 1.0, match)
        gate = jnp.where(hit, gates_t[k : k + 1, :], gate)
    before = lax.broadcasted_iota(jnp.int32, (toks, toks), 0) < lax.broadcasted_iota(
        jnp.int32, (toks, toks), 1
    )
    rank = jnp.dot(match.astype(BF16), before.astype(BF16), preferred_element_type=F32)
    chosen = (match > 0.5) & (rank.astype(jnp.int32) == slot) & allowed
    return chosen, jnp.where(chosen, gate, 0.0)


def expert_of(dev, member, devs, halves, cores, members):
    cell = dev // halves
    depth = devs // halves
    pair = dev % halves * depth + cell % cores * (depth // cores) + cell // cores
    return pair * members + member


def main_rows(member, toks, devs, halves, cores, members):
    row = lax.broadcasted_iota(jnp.int32, (devs * MAIN, toks), 0)
    return expert_of(row // MAIN, member, devs, halves, cores, members), row % MAIN


def tail_rows(toks, devs, halves, cores, members):
    row = lax.broadcasted_iota(jnp.int32, (devs * TAIL, toks), 0)
    dev, place = row // TAIL, row % TAIL
    return expert_of(dev, place % members, devs, halves, cores, members), place // members


def pack_kernel(gate_ref, up_ref, down_ref, *packed):
    for member, ref in enumerate(packed):
        for which, weight in enumerate((gate_ref, up_ref, down_ref)):
            ref[which] = weight[member]


def send_kernel(halves, cores, members, routes_ref, gates_ref, tok_ref, grad_ref, *outs):
    send_ref, hot_ref, high_ref, low_ref, hot_tail_ref, high_tail_ref, low_tail_ref = outs
    devs, _, width = send_ref.shape
    toks = tok_ref.shape[0]
    routes_t, gates_t = routes_ref[...], gates_ref[...]
    tok, grad = tok_ref[...], grad_ref[...]
    for member in range(members):
        expert, slot = main_rows(member, toks, devs, halves, cores, members)
        chosen, gate = picks(routes_t, gates_t, expert, slot, True)
        hot = chosen.astype(F32).astype(BF16)
        put(send_ref, member, jnp.dot(hot, tok, preferred_element_type=F32).astype(BF16))
        scale = jnp.sum(gate, axis=1, keepdims=True)
        rows = scale * jnp.dot(hot, grad, preferred_element_type=F32)
        put(send_ref, members + member, rows.astype(BF16))
        hot_ref[member] = hot
        high_ref[member], low_ref[member] = split(gate)
    expert, kind = tail_rows(toks, devs, halves, cores, members)
    chosen, gate = picks(routes_t, gates_t, expert, MAIN, kind < 2)
    hot = chosen.astype(F32)
    scale = jnp.sum(gate, axis=1, keepdims=True)
    hot_x = jnp.where(kind == 0, hot, 0.0).astype(BF16)
    hot_p = jnp.where(kind == 1, hot, 0.0).astype(BF16)
    rows = jnp.dot(hot_x, tok, preferred_element_type=F32) + scale * jnp.dot(
        hot_p, grad, preferred_element_type=F32
    )
    put_tail(send_ref, rows.astype(BF16))
    hot_tail_ref[0], hot_tail_ref[1] = hot_x, hot_p
    high_tail_ref[...], low_tail_ref[...] = split(jnp.where(kind == 0, gate, 0.0))


def put(ref, place, rows):
    ref[:, place * MAIN : (place + 1) * MAIN, :] = rows.reshape(-1, MAIN, rows.shape[-1])


def put_tail(ref, rows):
    ref[:, ref.shape[1] - TAIL :, :] = rows.reshape(-1, TAIL, rows.shape[-1])


def take(ref, place):
    return ref[:, place * MAIN : (place + 1) * MAIN, :].reshape(-1, ref.shape[-1])


def take_tail(ref):
    return ref[:, ref.shape[1] - TAIL :, :].reshape(-1, ref.shape[-1])


def tail_order(devs, members):
    shape = (2 * members * devs, devs * TAIL)
    row = lax.broadcasted_iota(jnp.int32, shape, 0)
    col = lax.broadcasted_iota(jnp.int32, shape, 1)
    return (col == row % devs * TAIL + row // devs).astype(F32).astype(BF16)


def tails_of(ref, members):
    order = tail_order(ref.shape[0], members)
    return jnp.dot(order, take_tail(ref), preferred_element_type=F32).astype(BF16)


def rows_of(ref, tails, place):
    devs = ref.shape[0]
    return jnp.concatenate([take(ref, place), tails[place * devs : (place + 1) * devs]], axis=0)


def fetch(sems, pairs):
    copies = [pltpu.make_async_copy(src, dst, sems.at[i]) for i, (src, dst) in enumerate(pairs)]
    for copy in copies:
        copy.start()
    return copies


def pieces(depth, cores, shift):
    near = depth // cores
    found = []
    for c in range(cores):
        at = (c * near + shift) % depth
        count = min(near, depth - at)
        found.append((c, 0, at, count))
        if count < near:
            found.append((c, count, 0, near - count))
    return found


def parts_of(w_hbm, member, shift, which, ref):
    return [
        (w_hbm.at[at : at + count, member, which], ref.at[cell : cell + count, c, member])
        for c, cell, at, count in pieces(w_hbm.shape[0], ref.shape[1], shift)
    ]


def matrix(ref, member):
    near, cores, _, rows, units = ref.shape
    return ref[:, :, member].reshape(near * cores * rows, units)


def sort_kernel(members, got_ref, x_ref, p_ref):
    tails = tails_of(got_ref, members)
    for member in range(members):
        x_ref[member] = rows_of(got_ref, tails, member)
        p_ref[member] = rows_of(got_ref, tails, members + member)


def arrive(sems, w_hbm, shifts, matrices):
    members = len(shifts)
    pairs, groups = [], []
    for member in range(members):
        found = [
            pair
            for which, ref in matrices
            for pair in parts_of(w_hbm, member, shifts[member], which, ref)
        ]
        groups.append(slice(len(pairs), len(pairs) + len(found)))
        pairs += found
    copies = fetch(sems, pairs)

    def wait(member):
        for copy in copies[groups[member]]:
            copy.wait()

    return wait


def hidden_kernel(shifts, x_ref, p_ref, w_hbm, part_ref, gate_ref, up_ref, sems):
    near, cores = gate_ref.shape[:2]
    weights_here = arrive(sems, w_hbm, shifts, ((0, gate_ref), (1, up_ref)))
    for member in range(len(shifts)):
        weights_here(member)
        rows = x_ref[member]
        pre_gate = jnp.dot(rows, matrix(gate_ref, member), preferred_element_type=F32)
        pre_up = jnp.dot(rows, matrix(up_ref, member), preferred_element_type=F32)
        active = pre_gate / (1.0 + jnp.exp(-pre_gate))
        hidden = (active * pre_up).astype(BF16)
        part = lax.dot_general(p_ref[member], hidden, FIRST, preferred_element_type=F32)
        part = part.reshape(near, cores, *part_ref.shape[2:])
        for c in range(cores):
            part_ref[c * near : (c + 1) * near, member] = part[:, c]


def rest_kernel(shifts, x_ref, p_ref, w_hbm, back_ref, gate_ref, up_ref, down_ref, sems):
    members = len(shifts)
    devs = back_ref.shape[0]
    weights_here = arrive(sems, w_hbm, shifts, ((0, gate_ref), (1, up_ref), (2, down_ref)))
    tails = [None] * (2 * members)
    for member in range(members):
        weights_here(member)
        rows = x_ref[member]
        gate_w, up_w, down_w = (matrix(ref, member) for ref in (gate_ref, up_ref, down_ref))
        pre_gate = jnp.dot(rows, gate_w, preferred_element_type=F32)
        pre_up = jnp.dot(rows, up_w, preferred_element_type=F32)
        squash = 1.0 / (1.0 + jnp.exp(-pre_gate))
        active = pre_gate * squash
        hidden = (active * pre_up).astype(BF16)
        out = lax.dot_general(hidden, down_w, LAST, preferred_element_type=F32).astype(BF16)
        put(back_ref, member, out[: devs * MAIN])
        tails[member] = out[devs * MAIN :]
        hidden_grad = jnp.dot(p_ref[member], down_w, preferred_element_type=F32)
        gate_pre = hidden_grad * pre_up * squash * (1.0 + pre_gate * (1.0 - squash))
        up_pre = hidden_grad * active
        grad = (
            lax.dot_general(gate_pre.astype(BF16), gate_w, LAST, preferred_element_type=F32)
            + lax.dot_general(up_pre.astype(BF16), up_w, LAST, preferred_element_type=F32)
        ).astype(BF16)
        put(back_ref, members + member, grad[: devs * MAIN])
        tails[members + member] = grad[devs * MAIN :]
    tails = jnp.concatenate(tails, axis=0)
    tails = lax.dot_general(tail_order(devs, members), tails, FIRST, preferred_element_type=F32)
    put_tail(back_ref, tails.astype(BF16))


def split(values):
    high = values.astype(BF16)
    return high, (values - high.astype(F32)).astype(BF16)


def gather(weights, rows):
    return lax.dot_general(weights, rows, FIRST, preferred_element_type=F32)


def by_choice(routes_t, expert, score):
    return [
        jnp.sum(jnp.where(expert == routes_t[k : k + 1, :], score, 0.0), axis=0, keepdims=True)
        for k in range(routes_t.shape[0])
    ]


def scores(chosen, rows, og):
    return jnp.where(chosen, lax.dot_general(rows, og, LAST, preferred_element_type=F32), 0.0)


def combine_kernel(halves, cores, members, routes_ref, grad_ref, *refs):
    hot_ref, high_ref, low_ref, hot_tail_ref, high_tail_ref, low_tail_ref = refs[:6]
    back_ref, mix_ref, in_ref, gg_ref = refs[6:]
    devs = back_ref.shape[0]
    routes_t, og = routes_ref[...], grad_ref[...]
    toks = og.shape[0]
    tail = take_tail(back_ref)
    expert, _ = tail_rows(toks, devs, halves, cores, members)
    lines = by_choice(routes_t, expert, scores(hot_tail_ref[0].astype(F32) > 0.5, tail, og))
    mix = gather(high_tail_ref[...], tail) + gather(low_tail_ref[...], tail)
    summed = gather(hot_tail_ref[1], tail)
    for member in range(members):
        out = take(back_ref, member)
        mix = mix + gather(high_ref[member], out) + gather(low_ref[member], out)
        summed = summed + gather(hot_ref[member], take(back_ref, members + member))
        expert, _ = main_rows(member, toks, devs, halves, cores, members)
        chosen = hot_ref[member].astype(F32) > 0.5
        more = by_choice(routes_t, expert, scores(chosen, out, og))
        lines = [a + b for a, b in zip(lines, more)]
    mix_ref[...] = mix.astype(BF16)
    in_ref[...] = summed.astype(BF16)
    for k, line in enumerate(lines):
        gg_ref[k : k + 1, :] = line


def call(kernel, name, outs, flops, args, anywhere=(), scratch=(), room=60, near=(), keep=False):
    flat = outs if isinstance(outs, tuple) else (outs,)
    total = sum(a.size * a.dtype.itemsize for a in (*args, *flat))
    inner = pl.BlockSpec()
    outer = pl.BlockSpec(memory_space=pltpu.HBM)
    held = pl.BlockSpec(memory_space=pltpu.VMEM)
    result = held if keep else inner
    return pl.pallas_call(
        kernel,
        name=name,
        out_shape=outs,
        in_specs=[outer if i in anywhere else held if i in near else inner for i in range(len(args))],
        out_specs=tuple(result for _ in flat) if isinstance(outs, tuple) else result,
        scratch_shapes=scratch,
        compiler_params=pltpu.CompilerParams(vmem_limit_bytes=room << 20),
        cost_estimate=pl.CostEstimate(flops=flops, bytes_accessed=total, transcendentals=0),
    )(*args)


def per_device(tokens, routes, gates, out_grad, w_gate, w_up, w_down):
    devs = lax.axis_size(PLANE)
    dp_devs = lax.axis_size(DP)
    halves = lax.axis_size("xh")
    cores = lax.axis_size("c")
    depth = lax.axis_size("z")
    toks, width = tokens.shape
    members, slice_rows, units = w_gate.shape
    side = members * MAIN
    slots = devs * (MAIN + 1)
    shape = jax.ShapeDtypeStruct
    vmem = pltpu.VMEM
    dma = pltpu.SemaphoreType.DMA
    near = dp_devs // cores

    def order(cell):
        return cell % cores * near + cell // cores

    def moves(shift):
        return [
            (cell * depth + order(other), other * depth + (order(cell) + shift) % depth)
            for cell in range(dp_devs)
            for other in range(dp_devs)
        ]

    shifts = [member * (depth // 4) for member in range(members)]
    axes = DP + ("z",)

    with jax.named_scope("weights"):
        each = shape((3, slice_rows, units), BF16)
        packed = call(
            pack_kernel, "pack", (each,) * members, 0, (w_gate, w_up, w_down.transpose(0, 2, 1))
        )
        packed = [lax.ppermute(w, axes, moves(shift)) for w, shift in zip(packed, shifts)]
        packed = jnp.stack(packed)

    with jax.named_scope("send"):
        routes_t, gates_t = routes.T, gates.T
        main = shape((members, devs * MAIN, toks), BF16)
        extra = shape((devs * TAIL, toks), BF16)
        rows, *who = call(
            functools.partial(send_kernel, halves, cores, members),
            "send",
            (
                shape((devs, 2 * side + TAIL, width), BF16),
                main,
                main,
                main,
                shape((2, devs * TAIL, toks), BF16),
                extra,
                extra,
            ),
            4 * slots * members * toks * width,
            (routes_t, gates_t, tokens, out_grad),
        )
        packed, rows = lax.optimization_barrier((packed, rows))
        full = lax.all_gather(packed, "z", axis=0)
        rows = swap(rows, PLANE)

    unit = 2 * slots * members * width * units
    held = vmem((near, cores, members, slice_rows, units), BF16)
    count = sum(len(pieces(depth, cores, shift)) for shift in shifts)
    with jax.named_scope("sort"):
        sorted_rows = shape((members, slots, width), BF16)
        x, piece = call(
            functools.partial(sort_kernel, members),
            "sort",
            (sorted_rows, sorted_rows),
            0,
            (rows,),
            room=56,
            keep=True,
        )

    with jax.named_scope("hidden"):
        part = call(
            functools.partial(hidden_kernel, shifts),
            "hidden",
            shape((depth, members, slice_rows, units), F32),
            3 * unit,
            (x, piece, full),
            (2,),
            (held, held, dma((2 * count,))),
            room=56,
            near=(0, 1),
        )
        full, part = lax.optimization_barrier((full, part))

    with jax.named_scope("down_grad"):
        part = lax.psum_scatter(part, "z", scatter_dimension=0)
        part = lax.ppermute(part.astype(BF16), axes, moves(0))

    with jax.named_scope("rest"):
        back = call(
            functools.partial(rest_kernel, shifts),
            "rest",
            shape(rows.shape, BF16),
            6 * unit,
            (x, piece, full),
            (2,),
            (held, held, held, dma((3 * count,))),
            room=56,
            near=(0, 1),
        )
        back = swap(back, PLANE)

    with jax.named_scope("combine"):
        mixed, input_grad, gate_grad = call(
            functools.partial(combine_kernel, halves, cores, members),
            "combine",
            (shape((toks, width), BF16), shape((toks, width), BF16), shape(routes_t.shape, F32)),
            8 * slots * members * toks * width,
            (routes_t, out_grad, *who, back),
            room=24,
        )

    with jax.named_scope("down_grad"):
        part, mixed = lax.optimization_barrier((part, mixed))
        down_grad = part.transpose(0, 2, 1).astype(F32)
    return (mixed, input_grad, gate_grad.T, down_grad)


def solution(mesh):
    fine = Mesh(mesh.devices.reshape(2, 4, 2, 2, 16), BLOCKS)
    rows = P(BLOCKS, None)
    return jax.shard_map(
        per_device,
        mesh=fine,
        in_specs=(
            rows,
            rows,
            rows,
            rows,
            P(("xh", "z"), DP, None),
            P(("xh", "z"), DP, None),
            P(("xh", "z"), None, DP),
        ),
        out_specs=(rows, rows, rows, P(("xh", "z"), None, DP)),
        check_vma=False,
    )
```

```python
import functools

import jax
import jax.numpy as jnp
from jax import lax
from jax.experimental import pallas as pl
from jax.experimental.pallas import tpu as pltpu
from jax.sharding import Mesh, PartitionSpec as P

DP = ("xl", "y", "c")
PLANE = ("xl", "y", "c", "xh")
BLOCKS = ("xl", "y", "c", "xh", "z")

MAIN = 16
ROOM = 50
TAIL = 8
F32 = jnp.float32
BF16 = jnp.bfloat16
LAST = (((1,), (1,)), ((), ()))
FIRST = (((0,), (0,)), ((), ()))


def swap(values, axes):
    return lax.all_to_all(values, axes, split_axis=0, concat_axis=0, tiled=True)


def picks(routes_t, gates_t, expert, slot, allowed):
    rows, toks = expert.shape
    match = jnp.zeros((rows, toks), F32)
    gate = jnp.zeros((rows, toks), F32)
    for k in range(routes_t.shape[0]):
        hit = expert == routes_t[k : k + 1, :]
        match = jnp.where(hit, 1.0, match)
        gate = jnp.where(hit, gates_t[k : k + 1, :], gate)
    before = lax.broadcasted_iota(jnp.int32, (toks, toks), 0) < lax.broadcasted_iota(
        jnp.int32, (toks, toks), 1
    )
    rank = jnp.dot(match.astype(BF16), before.astype(BF16), preferred_element_type=F32)
    chosen = (match > 0.5) & (rank.astype(jnp.int32) == slot) & allowed
    return chosen, jnp.where(chosen, gate, 0.0)


def expert_of(dev, member, devs, halves, cores, members):
    cell = dev // halves
    depth = devs // halves
    pair = dev % halves * depth + cell % cores * (depth // cores) + cell // cores
    return pair * members + member


def main_rows(member, toks, devs, halves, cores, members):
    row = lax.broadcasted_iota(jnp.int32, (devs * MAIN, toks), 0)
    return expert_of(row // MAIN, member, devs, halves, cores, members), row % MAIN


def tail_rows(toks, devs, halves, cores, members):
    row = lax.broadcasted_iota(jnp.int32, (devs * TAIL, toks), 0)
    dev, place = row // TAIL, row % TAIL
    return expert_of(dev, place % members, devs, halves, cores, members), place // members


def pack_kernel(gate_ref, up_ref, down_ref, *packed):
    for member, ref in enumerate(packed):
        for which, weight in enumerate((gate_ref, up_ref, down_ref)):
            ref[which] = weight[member]


def send_kernel(halves, cores, members, routes_ref, gates_ref, tok_ref, grad_ref, *outs):
    send_ref, hot_ref, high_ref, low_ref, hot_tail_ref, high_tail_ref, low_tail_ref = outs
    devs, _, width = send_ref.shape
    toks = tok_ref.shape[0]
    routes_t, gates_t = routes_ref[...], gates_ref[...]
    tok, grad = tok_ref[...], grad_ref[...]
    for member in range(members):
        expert, slot = main_rows(member, toks, devs, halves, cores, members)
        chosen, gate = picks(routes_t, gates_t, expert, slot, True)
        hot = chosen.astype(F32).astype(BF16)
        put(send_ref, member, jnp.dot(hot, tok, preferred_element_type=F32).astype(BF16))
        scale = jnp.sum(gate, axis=1, keepdims=True)
        rows = scale * jnp.dot(hot, grad, preferred_element_type=F32)
        put(send_ref, members + member, rows.astype(BF16))
        hot_ref[member] = hot
        high_ref[member], low_ref[member] = split(gate)
    expert, kind = tail_rows(toks, devs, halves, cores, members)
    chosen, gate = picks(routes_t, gates_t, expert, MAIN, kind < 2)
    hot = chosen.astype(F32)
    scale = jnp.sum(gate, axis=1, keepdims=True)
    hot_x = jnp.where(kind == 0, hot, 0.0).astype(BF16)
    hot_p = jnp.where(kind == 1, hot, 0.0).astype(BF16)
    rows = jnp.dot(hot_x, tok, preferred_element_type=F32) + scale * jnp.dot(
        hot_p, grad, preferred_element_type=F32
    )
    put_tail(send_ref, rows.astype(BF16))
    hot_tail_ref[0], hot_tail_ref[1] = hot_x, hot_p
    high_tail_ref[...], low_tail_ref[...] = split(jnp.where(kind == 0, gate, 0.0))


def put(ref, place, rows):
    ref[:, place * MAIN : (place + 1) * MAIN, :] = rows.reshape(-1, MAIN, rows.shape[-1])


def put_tail(ref, rows):
    ref[:, ref.shape[1] - TAIL :, :] = rows.reshape(-1, TAIL, rows.shape[-1])


def take(ref, place):
    return ref[:, place * MAIN : (place + 1) * MAIN, :].reshape(-1, ref.shape[-1])


def take_tail(ref):
    return ref[:, ref.shape[1] - TAIL :, :].reshape(-1, ref.shape[-1])


def tail_order(devs, members):
    shape = (2 * members * devs, devs * TAIL)
    row = lax.broadcasted_iota(jnp.int32, shape, 0)
    col = lax.broadcasted_iota(jnp.int32, shape, 1)
    return (col == row % devs * TAIL + row // devs).astype(F32).astype(BF16)


def tails_of(ref, members):
    order = tail_order(ref.shape[0], members)
    return jnp.dot(order, take_tail(ref), preferred_element_type=F32).astype(BF16)


def rows_of(ref, tails, place):
    devs = ref.shape[0]
    return jnp.concatenate([take(ref, place), tails[place * devs : (place + 1) * devs]], axis=0)


def fetch(sems, pairs):
    copies = [pltpu.make_async_copy(src, dst, sems.at[i]) for i, (src, dst) in enumerate(pairs)]
    for copy in copies:
        copy.start()
    return copies


def pieces(depth, cores, shift):
    near = depth // cores
    found = []
    for c in range(cores):
        at = (c * near + shift) % depth
        count = min(near, depth - at)
        found.append((c, 0, at, count))
        if count < near:
            found.append((c, count, 0, near - count))
    return found


def parts_of(w_hbm, member, shift, which, ref):
    return [
        (w_hbm.at[at : at + count, member, which], ref.at[cell : cell + count, c, member])
        for c, cell, at, count in pieces(w_hbm.shape[0], ref.shape[1], shift)
    ]


def matrix(ref, member):
    near, cores, _, rows, units = ref.shape
    return ref[:, :, member].reshape(near * cores * rows, units)


def sort_kernel(members, got_ref, x_ref, p_ref, turned_ref):
    tails = tails_of(got_ref, members)
    for member in range(members):
        x_ref[member] = rows_of(got_ref, tails, member)
        piece = rows_of(got_ref, tails, members + member)
        p_ref[member] = piece
        turned_ref[member] = piece.T


def arrive(sems, w_hbm, shifts, matrices):
    members = len(shifts)
    pairs, groups = [], []
    for member in range(members):
        found = [
            pair
            for which, ref in matrices
            for pair in parts_of(w_hbm, member, shifts[member], which, ref)
        ]
        groups.append(slice(len(pairs), len(pairs) + len(found)))
        pairs += found
    copies = fetch(sems, pairs)

    def wait(member):
        for copy in copies[groups[member]]:
            copy.wait()

    return wait


def hidden_kernel(shifts, x_ref, turned_ref, w_hbm, part_hbm, gate_out_ref, up_out_ref, *scratch):
    hold_ref, gate_ref, up_ref, sems, out_sems = scratch
    near, cores = gate_ref.shape[:2]
    weights_here = arrive(sems, w_hbm, shifts, ((0, gate_ref), (1, up_ref)))
    sent = []
    for member in range(len(shifts)):
        weights_here(member)
        rows = x_ref[member]
        pre_gate = jnp.dot(rows, matrix(gate_ref, member), preferred_element_type=F32)
        pre_up = jnp.dot(rows, matrix(up_ref, member), preferred_element_type=F32)
        squash = 1.0 / (1.0 + jnp.exp(-pre_gate))
        active = pre_gate * squash
        hidden = (active * pre_up).astype(BF16)
        part = jnp.dot(turned_ref[member], hidden, preferred_element_type=F32)
        hold_ref[member] = part.reshape(hold_ref.shape[1:])
        for c in range(cores):
            copy = pltpu.make_async_copy(
                hold_ref.at[member, :, c],
                part_hbm.at[c * near : (c + 1) * near, member],
                out_sems.at[member, c],
            )
            copy.start()
            sent.append(copy)
        gate_out_ref[member] = pre_gate
        up_out_ref[member] = pre_up
    for copy in sent:
        copy.wait()


def rest_kernel(shifts, x_ref, y_ref, p_ref, w_hbm, back_ref, gate_ref, up_ref, down_ref, sems):
    members = len(shifts)
    devs = back_ref.shape[0]
    weights_here = arrive(sems, w_hbm, shifts, ((2, down_ref), (0, gate_ref), (1, up_ref)))
    tails = [None] * (2 * members)
    for member in range(members):
        weights_here(member)
        gate_w, up_w, down_w = (matrix(ref, member) for ref in (gate_ref, up_ref, down_ref))
        pre_gate, pre_up = x_ref[member], y_ref[member]
        squash = 1.0 / (1.0 + jnp.exp(-pre_gate))
        active = pre_gate * squash
        hidden = (active * pre_up).astype(BF16)
        out = lax.dot_general(hidden, down_w, LAST, preferred_element_type=F32).astype(BF16)
        put(back_ref, member, out[: devs * MAIN])
        tails[member] = out[devs * MAIN :]
        hidden_grad = jnp.dot(p_ref[member], down_w, preferred_element_type=F32)
        gate_pre = hidden_grad * pre_up * squash * (1.0 + pre_gate * (1.0 - squash))
        up_pre = hidden_grad * active
        grad = (
            lax.dot_general(gate_pre.astype(BF16), gate_w, LAST, preferred_element_type=F32)
            + lax.dot_general(up_pre.astype(BF16), up_w, LAST, preferred_element_type=F32)
        ).astype(BF16)
        put(back_ref, members + member, grad[: devs * MAIN])
        tails[members + member] = grad[devs * MAIN :]
    tails = jnp.concatenate(tails, axis=0)
    tails = lax.dot_general(tail_order(devs, members), tails, FIRST, preferred_element_type=F32)
    put_tail(back_ref, tails.astype(BF16))


def split(values):
    high = values.astype(BF16)
    return high, (values - high.astype(F32)).astype(BF16)


def gather(weights, rows):
    return lax.dot_general(weights, rows, FIRST, preferred_element_type=F32)


def by_choice(routes_t, expert, score):
    return [
        jnp.sum(jnp.where(expert == routes_t[k : k + 1, :], score, 0.0), axis=0, keepdims=True)
        for k in range(routes_t.shape[0])
    ]


def scores(chosen, rows, og):
    return jnp.where(chosen, lax.dot_general(rows, og, LAST, preferred_element_type=F32), 0.0)


def combine_kernel(halves, cores, members, routes_ref, grad_ref, *refs):
    hot_ref, high_ref, low_ref, hot_tail_ref, high_tail_ref, low_tail_ref = refs[:6]
    back_ref, mix_ref, in_ref, gg_ref = refs[6:]
    devs = back_ref.shape[0]
    routes_t, og = routes_ref[...], grad_ref[...]
    toks = og.shape[0]
    tail = take_tail(back_ref)
    expert, _ = tail_rows(toks, devs, halves, cores, members)
    lines = by_choice(routes_t, expert, scores(hot_tail_ref[0].astype(F32) > 0.5, tail, og))
    mix = gather(high_tail_ref[...], tail) + gather(low_tail_ref[...], tail)
    summed = gather(hot_tail_ref[1], tail)
    for member in range(members):
        out = take(back_ref, member)
        mix = mix + gather(high_ref[member], out) + gather(low_ref[member], out)
        summed = summed + gather(hot_ref[member], take(back_ref, members + member))
        expert, _ = main_rows(member, toks, devs, halves, cores, members)
        chosen = hot_ref[member].astype(F32) > 0.5
        more = by_choice(routes_t, expert, scores(chosen, out, og))
        lines = [a + b for a, b in zip(lines, more)]
    mix_ref[...] = mix.astype(BF16)
    in_ref[...] = summed.astype(BF16)
    for k, line in enumerate(lines):
        gg_ref[k : k + 1, :] = line


def call(kernel, name, outs, flops, args, anywhere=(), scratch=(), room=60, near=(), keep=False, apart=()):
    flat = outs if isinstance(outs, tuple) else (outs,)
    total = sum(a.size * a.dtype.itemsize for a in (*args, *flat))
    inner = pl.BlockSpec()
    outer = pl.BlockSpec(memory_space=pltpu.HBM)
    held = pl.BlockSpec(memory_space=pltpu.VMEM)
    results = [outer if i in apart else held if keep else inner for i in range(len(flat))]
    return pl.pallas_call(
        kernel,
        name=name,
        out_shape=outs,
        in_specs=[outer if i in anywhere else held if i in near else inner for i in range(len(args))],
        out_specs=tuple(results) if isinstance(outs, tuple) else results[0],
        scratch_shapes=scratch,
        compiler_params=pltpu.CompilerParams(vmem_limit_bytes=room << 20),
        cost_estimate=pl.CostEstimate(flops=flops, bytes_accessed=total, transcendentals=0),
    )(*args)


def per_device(tokens, routes, gates, out_grad, w_gate, w_up, w_down):
    devs = lax.axis_size(PLANE)
    dp_devs = lax.axis_size(DP)
    halves = lax.axis_size("xh")
    cores = lax.axis_size("c")
    depth = lax.axis_size("z")
    toks, width = tokens.shape
    members, slice_rows, units = w_gate.shape
    side = members * MAIN
    slots = devs * (MAIN + 1)
    shape = jax.ShapeDtypeStruct
    vmem = pltpu.VMEM
    dma = pltpu.SemaphoreType.DMA
    near = dp_devs // cores

    def order(cell):
        return cell % cores * near + cell // cores

    def moves(shift):
        return [
            (cell * depth + order(other), other * depth + (order(cell) + shift) % depth)
            for cell in range(dp_devs)
            for other in range(dp_devs)
        ]

    shifts = [member * (depth // 4) for member in range(members)]
    axes = DP + ("z",)

    with jax.named_scope("weights"):
        each = shape((3, slice_rows, units), BF16)
        packed = call(
            pack_kernel, "pack", (each,) * members, 0, (w_gate, w_up, w_down.transpose(0, 2, 1))
        )
        packed = [lax.ppermute(w, axes, moves(shift)) for w, shift in zip(packed, shifts)]
        packed = jnp.stack(packed)

    with jax.named_scope("send"):
        routes_t, gates_t = routes.T, gates.T
        main = shape((members, devs * MAIN, toks), BF16)
        extra = shape((devs * TAIL, toks), BF16)
        rows, *who = call(
            functools.partial(send_kernel, halves, cores, members),
            "send",
            (
                shape((devs, 2 * side + TAIL, width), BF16),
                main,
                main,
                main,
                shape((2, devs * TAIL, toks), BF16),
                extra,
                extra,
            ),
            4 * slots * members * toks * width,
            (routes_t, gates_t, tokens, out_grad),
        )
        packed, rows = lax.optimization_barrier((packed, rows))
        full = lax.all_gather(packed, "z", axis=0)
        rows = swap(rows, PLANE)

    unit = 2 * slots * members * width * units
    held = vmem((near, cores, members, slice_rows, units), BF16)
    count = sum(len(pieces(depth, cores, shift)) for shift in shifts)
    with jax.named_scope("sort"):
        ordered = shape((members, slots, width), BF16)
        x, piece, turned = call(
            functools.partial(sort_kernel, members),
            "sort",
            (ordered, ordered, shape((members, width, slots), BF16)),
            0,
            (rows,),
            room=ROOM,
            keep=True,
        )

    with jax.named_scope("hidden"):
        wide = shape((members, slots, units), F32)
        part, pre_gate, pre_up = call(
            functools.partial(hidden_kernel, shifts),
            "hidden",
            (shape((depth, members, slice_rows, units), F32), wide, wide),
            3 * unit,
            (x, turned, full),
            (2,),
            (
                vmem((members, near, cores, slice_rows, units), F32),
                held,
                held,
                dma((2 * count,)),
                dma((members, cores)),
            ),
            room=ROOM,
            near=(0, 1),
            keep=True,
            apart=(0,),
        )

    with jax.named_scope("down_grad"):
        part = lax.psum_scatter(part, "z", scatter_dimension=0)
        part = lax.ppermute(part.astype(BF16), axes, moves(0))

    with jax.named_scope("rest"):
        back = call(
            functools.partial(rest_kernel, shifts),
            "rest",
            shape(rows.shape, BF16),
            4 * unit,
            (pre_gate, pre_up, piece, full),
            (3,),
            (held, held, held, dma((3 * count,))),
            room=ROOM,
            near=(0, 1, 2),
        )
        back = swap(back, PLANE)

    with jax.named_scope("combine"):
        mixed, input_grad, gate_grad = call(
            functools.partial(combine_kernel, halves, cores, members),
            "combine",
            (shape((toks, width), BF16), shape((toks, width), BF16), shape(routes_t.shape, F32)),
            8 * slots * members * toks * width,
            (routes_t, out_grad, *who, back),
            room=24,
        )

    with jax.named_scope("down_grad"):
        part, mixed = lax.optimization_barrier((part, mixed))
        down_grad = part.transpose(0, 2, 1).astype(F32)
    return (mixed, input_grad, gate_grad.T, down_grad)


def solution(mesh):
    fine = Mesh(mesh.devices.reshape(2, 4, 2, 2, 16), BLOCKS)
    rows = P(BLOCKS, None)
    return jax.shard_map(
        per_device,
        mesh=fine,
        in_specs=(
            rows,
            rows,
            rows,
            rows,
            P(("xh", "z"), DP, None),
            P(("xh", "z"), DP, None),
            P(("xh", "z"), None, DP),
        ),
        out_specs=(rows, rows, rows, P(("xh", "z"), None, DP)),
        check_vma=False,
    )
```

```python
import functools

import jax
import jax.numpy as jnp
from jax import lax
from jax.experimental import pallas as pl
from jax.experimental.pallas import tpu as pltpu
from jax.sharding import Mesh, PartitionSpec as P

DP = ("xl", "y", "c")
PLANE = ("xl", "y", "c", "xh")
BLOCKS = ("xl", "y", "c", "xh", "z")

MAIN = 16
ROOM = 50
TAIL = 8
F32 = jnp.float32
BF16 = jnp.bfloat16
LAST = (((1,), (1,)), ((), ()))
FIRST = (((0,), (0,)), ((), ()))


def swap(values, axes):
    return lax.all_to_all(values, axes, split_axis=0, concat_axis=0, tiled=True)


def picks(routes_t, gates_t, expert, slot, allowed):
    rows, toks = expert.shape
    match = jnp.zeros((rows, toks), F32)
    gate = jnp.zeros((rows, toks), F32)
    for k in range(routes_t.shape[0]):
        hit = expert == routes_t[k : k + 1, :]
        match = jnp.where(hit, 1.0, match)
        gate = jnp.where(hit, gates_t[k : k + 1, :], gate)
    before = lax.broadcasted_iota(jnp.int32, (toks, toks), 0) < lax.broadcasted_iota(
        jnp.int32, (toks, toks), 1
    )
    rank = jnp.dot(match.astype(BF16), before.astype(BF16), preferred_element_type=F32)
    chosen = (match > 0.5) & (rank.astype(jnp.int32) == slot) & allowed
    return chosen, jnp.where(chosen, gate, 0.0)


def expert_of(dev, member, devs, halves, cores, members):
    cell = dev // halves
    depth = devs // halves
    pair = dev % halves * depth + cell % cores * (depth // cores) + cell // cores
    return pair * members + member


def main_rows(member, toks, devs, halves, cores, members):
    row = lax.broadcasted_iota(jnp.int32, (devs * MAIN, toks), 0)
    return expert_of(row // MAIN, member, devs, halves, cores, members), row % MAIN


def tail_rows(toks, devs, halves, cores, members):
    row = lax.broadcasted_iota(jnp.int32, (devs * TAIL, toks), 0)
    dev, place = row // TAIL, row % TAIL
    return expert_of(dev, place % members, devs, halves, cores, members), place // members


def pack_kernel(gate_ref, up_ref, down_ref, *packed):
    for member, ref in enumerate(packed):
        for which, weight in enumerate((gate_ref, up_ref, down_ref)):
            ref[which] = weight[member]


def send_kernel(halves, cores, members, routes_ref, gates_ref, tok_ref, grad_ref, *outs):
    send_ref, hot_ref, high_ref, low_ref, hot_tail_ref, high_tail_ref, low_tail_ref = outs
    devs, _, width = send_ref.shape
    toks = tok_ref.shape[0]
    routes_t, gates_t = routes_ref[...], gates_ref[...]
    tok, grad = tok_ref[...], grad_ref[...]
    for member in range(members):
        expert, slot = main_rows(member, toks, devs, halves, cores, members)
        chosen, gate = picks(routes_t, gates_t, expert, slot, True)
        hot = chosen.astype(F32).astype(BF16)
        put(send_ref, member, jnp.dot(hot, tok, preferred_element_type=F32).astype(BF16))
        scale = jnp.sum(gate, axis=1, keepdims=True)
        rows = scale * jnp.dot(hot, grad, preferred_element_type=F32)
        put(send_ref, members + member, rows.astype(BF16))
        hot_ref[member] = hot
        high_ref[member], low_ref[member] = split(gate)
    expert, kind = tail_rows(toks, devs, halves, cores, members)
    chosen, gate = picks(routes_t, gates_t, expert, MAIN, kind < 2)
    hot = chosen.astype(F32)
    scale = jnp.sum(gate, axis=1, keepdims=True)
    hot_x = jnp.where(kind == 0, hot, 0.0).astype(BF16)
    hot_p = jnp.where(kind == 1, hot, 0.0).astype(BF16)
    rows = jnp.dot(hot_x, tok, preferred_element_type=F32) + scale * jnp.dot(
        hot_p, grad, preferred_element_type=F32
    )
    put_tail(send_ref, rows.astype(BF16))
    hot_tail_ref[0], hot_tail_ref[1] = hot_x, hot_p
    high_tail_ref[...], low_tail_ref[...] = split(jnp.where(kind == 0, gate, 0.0))


def put(ref, place, rows):
    ref[:, place * MAIN : (place + 1) * MAIN, :] = rows.reshape(-1, MAIN, rows.shape[-1])


def put_tail(ref, rows):
    ref[:, ref.shape[1] - TAIL :, :] = rows.reshape(-1, TAIL, rows.shape[-1])


def take(ref, place):
    return ref[:, place * MAIN : (place + 1) * MAIN, :].reshape(-1, ref.shape[-1])


def take_tail(ref):
    return ref[:, ref.shape[1] - TAIL :, :].reshape(-1, ref.shape[-1])


def tail_order(devs, members):
    shape = (2 * members * devs, devs * TAIL)
    row = lax.broadcasted_iota(jnp.int32, shape, 0)
    col = lax.broadcasted_iota(jnp.int32, shape, 1)
    return (col == row % devs * TAIL + row // devs).astype(F32).astype(BF16)


def tails_of(ref, members):
    order = tail_order(ref.shape[0], members)
    return jnp.dot(order, take_tail(ref), preferred_element_type=F32).astype(BF16)


def rows_of(ref, tails, place):
    devs = ref.shape[0]
    return jnp.concatenate([take(ref, place), tails[place * devs : (place + 1) * devs]], axis=0)


def fetch(sems, pairs):
    copies = [pltpu.make_async_copy(src, dst, sems.at[i]) for i, (src, dst) in enumerate(pairs)]
    for copy in copies:
        copy.start()
    return copies


def pieces(depth, cores, shift):
    near = depth // cores
    found = []
    for c in range(cores):
        at = (c * near + shift) % depth
        count = min(near, depth - at)
        found.append((c, 0, at, count))
        if count < near:
            found.append((c, count, 0, near - count))
    return found


def parts_of(w_hbm, member, shift, which, ref, lane):
    units = w_hbm.shape[-1]
    return [
        (
            w_hbm.at[at : at + count, member, which],
            ref.at[cell : cell + count, c, member, :, lane * units : (lane + 1) * units],
        )
        for c, cell, at, count in pieces(w_hbm.shape[0], ref.shape[1], shift)
    ]


def matrix(ref, member):
    near, cores, _, rows, units = ref.shape
    return ref[:, :, member].reshape(near * cores * rows, units)


def sort_kernel(members, got_ref, x_ref, p_ref, turned_ref):
    tails = tails_of(got_ref, members)
    for member in range(members):
        x_ref[member] = rows_of(got_ref, tails, member)
        piece = rows_of(got_ref, tails, members + member)
        p_ref[member] = piece
        turned_ref[member] = piece.T


def arrive(sems, w_hbm, shifts, matrices):
    members = len(shifts)
    pairs, groups = [], []
    for member in range(members):
        found = [
            pair
            for which, ref, lane in matrices
            for pair in parts_of(w_hbm, member, shifts[member], which, ref, lane)
        ]
        groups.append(slice(len(pairs), len(pairs) + len(found)))
        pairs += found
    copies = fetch(sems, pairs)

    def wait(member):
        for copy in copies[groups[member]]:
            copy.wait()

    return wait


def hidden_kernel(shifts, x_ref, turned_ref, w_hbm, part_hbm, gate_out_ref, up_out_ref, *scratch):
    hold_ref, both_ref, sems, out_sems = scratch
    near, cores = both_ref.shape[:2]
    units = w_hbm.shape[-1]
    weights_here = arrive(sems, w_hbm, shifts, ((0, both_ref, 0), (1, both_ref, 1)))
    sent = []
    for member in range(len(shifts)):
        weights_here(member)
        pre = jnp.dot(x_ref[member], matrix(both_ref, member), preferred_element_type=F32)
        pre_gate, pre_up = pre[:, :units], pre[:, units:]
        squash = 1.0 / (1.0 + jnp.exp(-pre_gate))
        active = pre_gate * squash
        hidden = (active * pre_up).astype(BF16)
        part = jnp.dot(turned_ref[member], hidden, preferred_element_type=F32)
        hold_ref[member] = part.reshape(hold_ref.shape[1:])
        for c in range(cores):
            copy = pltpu.make_async_copy(
                hold_ref.at[member, :, c],
                part_hbm.at[c * near : (c + 1) * near, member],
                out_sems.at[member, c],
            )
            copy.start()
            sent.append(copy)
        gate_out_ref[member] = pre_gate
        up_out_ref[member] = pre_up
    for copy in sent:
        copy.wait()


def rest_kernel(shifts, x_ref, y_ref, p_ref, w_hbm, back_ref, both_ref, down_ref, sems):
    members = len(shifts)
    devs = back_ref.shape[0]
    weights_here = arrive(
        sems, w_hbm, shifts, ((2, down_ref, 0), (0, both_ref, 0), (1, both_ref, 1))
    )
    tails = [None] * (2 * members)
    for member in range(members):
        weights_here(member)
        down_w = matrix(down_ref, member)
        pre_gate, pre_up = x_ref[member], y_ref[member]
        squash = 1.0 / (1.0 + jnp.exp(-pre_gate))
        active = pre_gate * squash
        hidden = (active * pre_up).astype(BF16)
        out = lax.dot_general(hidden, down_w, LAST, preferred_element_type=F32).astype(BF16)
        put(back_ref, member, out[: devs * MAIN])
        tails[member] = out[devs * MAIN :]
        hidden_grad = jnp.dot(p_ref[member], down_w, preferred_element_type=F32)
        gate_pre = hidden_grad * pre_up * squash * (1.0 + pre_gate * (1.0 - squash))
        up_pre = hidden_grad * active
        pre = jnp.concatenate([gate_pre.astype(BF16), up_pre.astype(BF16)], axis=1)
        grad = lax.dot_general(
            pre, matrix(both_ref, member), LAST, preferred_element_type=F32
        ).astype(BF16)
        put(back_ref, members + member, grad[: devs * MAIN])
        tails[members + member] = grad[devs * MAIN :]
    tails = jnp.concatenate(tails, axis=0)
    tails = lax.dot_general(tail_order(devs, members), tails, FIRST, preferred_element_type=F32)
    put_tail(back_ref, tails.astype(BF16))


def split(values):
    high = values.astype(BF16)
    return high, (values - high.astype(F32)).astype(BF16)


def gather(weights, rows):
    return lax.dot_general(weights, rows, FIRST, preferred_element_type=F32)


def by_choice(routes_t, expert, score):
    return [
        jnp.sum(jnp.where(expert == routes_t[k : k + 1, :], score, 0.0), axis=0, keepdims=True)
        for k in range(routes_t.shape[0])
    ]


def scores(chosen, rows, og):
    return jnp.where(chosen, lax.dot_general(rows, og, LAST, preferred_element_type=F32), 0.0)


def combine_kernel(halves, cores, members, routes_ref, grad_ref, *refs):
    hot_ref, high_ref, low_ref, hot_tail_ref, high_tail_ref, low_tail_ref = refs[:6]
    back_ref, mix_ref, in_ref, gg_ref = refs[6:]
    devs = back_ref.shape[0]
    routes_t, og = routes_ref[...], grad_ref[...]
    toks = og.shape[0]
    tail = take_tail(back_ref)
    expert, _ = tail_rows(toks, devs, halves, cores, members)
    lines = by_choice(routes_t, expert, scores(hot_tail_ref[0].astype(F32) > 0.5, tail, og))
    mix = gather(high_tail_ref[...], tail) + gather(low_tail_ref[...], tail)
    summed = gather(hot_tail_ref[1], tail)
    for member in range(members):
        out = take(back_ref, member)
        mix = mix + gather(high_ref[member], out) + gather(low_ref[member], out)
        summed = summed + gather(hot_ref[member], take(back_ref, members + member))
        expert, _ = main_rows(member, toks, devs, halves, cores, members)
        chosen = hot_ref[member].astype(F32) > 0.5
        more = by_choice(routes_t, expert, scores(chosen, out, og))
        lines = [a + b for a, b in zip(lines, more)]
    mix_ref[...] = mix.astype(BF16)
    in_ref[...] = summed.astype(BF16)
    for k, line in enumerate(lines):
        gg_ref[k : k + 1, :] = line


def call(kernel, name, outs, flops, args, anywhere=(), scratch=(), room=60, near=(), keep=False, apart=()):
    flat = outs if isinstance(outs, tuple) else (outs,)
    total = sum(a.size * a.dtype.itemsize for a in (*args, *flat))
    inner = pl.BlockSpec()
    outer = pl.BlockSpec(memory_space=pltpu.HBM)
    held = pl.BlockSpec(memory_space=pltpu.VMEM)
    results = [outer if i in apart else held if keep else inner for i in range(len(flat))]
    return pl.pallas_call(
        kernel,
        name=name,
        out_shape=outs,
        in_specs=[outer if i in anywhere else held if i in near else inner for i in range(len(args))],
        out_specs=tuple(results) if isinstance(outs, tuple) else results[0],
        scratch_shapes=scratch,
        compiler_params=pltpu.CompilerParams(vmem_limit_bytes=room << 20),
        cost_estimate=pl.CostEstimate(flops=flops, bytes_accessed=total, transcendentals=0),
    )(*args)


def per_device(tokens, routes, gates, out_grad, w_gate, w_up, w_down):
    devs = lax.axis_size(PLANE)
    dp_devs = lax.axis_size(DP)
    halves = lax.axis_size("xh")
    cores = lax.axis_size("c")
    depth = lax.axis_size("z")
    toks, width = tokens.shape
    members, slice_rows, units = w_gate.shape
    side = members * MAIN
    slots = devs * (MAIN + 1)
    shape = jax.ShapeDtypeStruct
    vmem = pltpu.VMEM
    dma = pltpu.SemaphoreType.DMA
    near = dp_devs // cores

    def order(cell):
        return cell % cores * near + cell // cores

    def moves(shift):
        return [
            (cell * depth + order(other), other * depth + (order(cell) + shift) % depth)
            for cell in range(dp_devs)
            for other in range(dp_devs)
        ]

    shifts = [member * (depth // 4) for member in range(members)]
    axes = DP + ("z",)

    with jax.named_scope("weights"):
        each = shape((3, slice_rows, units), BF16)
        packed = call(
            pack_kernel, "pack", (each,) * members, 0, (w_gate, w_up, w_down.transpose(0, 2, 1))
        )
        packed = [lax.ppermute(w, axes, moves(shift)) for w, shift in zip(packed, shifts)]
        packed = jnp.stack(packed)

    with jax.named_scope("send"):
        routes_t, gates_t = routes.T, gates.T
        main = shape((members, devs * MAIN, toks), BF16)
        extra = shape((devs * TAIL, toks), BF16)
        rows, *who = call(
            functools.partial(send_kernel, halves, cores, members),
            "send",
            (
                shape((devs, 2 * side + TAIL, width), BF16),
                main,
                main,
                main,
                shape((2, devs * TAIL, toks), BF16),
                extra,
                extra,
            ),
            4 * slots * members * toks * width,
            (routes_t, gates_t, tokens, out_grad),
        )
        packed, rows = lax.optimization_barrier((packed, rows))
        full = lax.all_gather(packed, "z", axis=0)
        rows = swap(rows, PLANE)

    unit = 2 * slots * members * width * units
    held = vmem((near, cores, members, slice_rows, units), BF16)
    both = vmem((near, cores, members, slice_rows, 2 * units), BF16)
    count = sum(len(pieces(depth, cores, shift)) for shift in shifts)
    with jax.named_scope("sort"):
        ordered = shape((members, slots, width), BF16)
        x, piece, turned = call(
            functools.partial(sort_kernel, members),
            "sort",
            (ordered, ordered, shape((members, width, slots), BF16)),
            0,
            (rows,),
            room=ROOM,
            keep=True,
        )

    with jax.named_scope("hidden"):
        wide = shape((members, slots, units), F32)
        part, pre_gate, pre_up = call(
            functools.partial(hidden_kernel, shifts),
            "hidden",
            (shape((depth, members, slice_rows, units), F32), wide, wide),
            3 * unit,
            (x, turned, full),
            (2,),
            (
                vmem((members, near, cores, slice_rows, units), F32),
                both,
                dma((2 * count,)),
                dma((members, cores)),
            ),
            room=ROOM,
            near=(0, 1),
            keep=True,
            apart=(0,),
        )

    with jax.named_scope("down_grad"):
        part = lax.psum_scatter(part, "z", scatter_dimension=0)
        part = lax.ppermute(part.astype(BF16), axes, moves(0))

    with jax.named_scope("rest"):
        back = call(
            functools.partial(rest_kernel, shifts),
            "rest",
            shape(rows.shape, BF16),
            4 * unit,
            (pre_gate, pre_up, piece, full),
            (3,),
            (both, held, dma((3 * count,))),
            room=ROOM,
            near=(0, 1, 2),
        )
        back = swap(back, PLANE)

    with jax.named_scope("combine"):
        mixed, input_grad, gate_grad = call(
            functools.partial(combine_kernel, halves, cores, members),
            "combine",
            (shape((toks, width), BF16), shape((toks, width), BF16), shape(routes_t.shape, F32)),
            8 * slots * members * toks * width,
            (routes_t, out_grad, *who, back),
            room=24,
        )

    with jax.named_scope("down_grad"):
        part, mixed = lax.optimization_barrier((part, mixed))
        down_grad = part.transpose(0, 2, 1).astype(F32)
    return (mixed, input_grad, gate_grad.T, down_grad)


def solution(mesh):
    fine = Mesh(mesh.devices.reshape(2, 4, 2, 2, 16), BLOCKS)
    rows = P(BLOCKS, None)
    return jax.shard_map(
        per_device,
        mesh=fine,
        in_specs=(
            rows,
            rows,
            rows,
            rows,
            P(("xh", "z"), DP, None),
            P(("xh", "z"), DP, None),
            P(("xh", "z"), None, DP),
        ),
        out_specs=(rows, rows, rows, P(("xh", "z"), None, DP)),
        check_vma=False,
    )
```
